128 devices in a mesh: node: 8 (over y, core), outer: 16 (over z, x).
Axes of the slice: x: 4, y: 4, z: 4, core: 2. Of those that a mesh axis runs over, the one named last changes fastest.
Arguments:
- embeddings: bfloat16 [393216, 1024], P(('node', 'outer')), may hold values from -6 to 6
- embedding_parent_index: int32 [393216], P(('node', 'outer')), may hold values from 0 to 511, as said below
- parent_slot: int32 [512], replicated, may hold values from 0 to 511, each once
- centroids: bfloat16 [128, 512, 1024], P(None, 'outer'), may hold values from -6 to 6
Outputs:
- new_children: float32 [128, 512, 1024], P('node', 'outer')
- new_parents: float32 [512, 1024], P('outer')
The draws below stay inside these ranges and needn't reach their ends.
Inputs may be any that keep to these rules, and one draw needn't show every extreme that they name: `embedding_parent_index`: within each device's 3072 rows the ids never fall; every parent has at least 3 and at most 12 rows on every device, and some parent has exactly 12 rows on every device. `parent_slot`: each slot once; slot s lies on index s // 32 of outer.
All inputs are finite; a program needn't handle non-finite values.
Results may differ from the reference program's by a relative error of at most 0.0029.
Values may be sent and summed in bfloat16 or wider, within the bound.
No kernel may reach another device: no remote copies, remote signals or barrier semaphores. Data moves between devices by JAX's collectives and lax.ppermute only.
A program may use at most 192 MiB of HBM per device.

```python
import jax
import jax.numpy as jnp
from jax import lax

D = 1024
K = 128
TOK_DEV = 3072
PARENTS = 512
TOKENS = 393216
CAPP = 12
MINP = 3
DEVICES = 128


def draw_embedding_parent_index(key, part):
    hot_parent = jax.random.randint(jax.random.fold_in(key, 7), (), 0, PARENTS, dtype=jnp.int32)
    device_keys = jax.random.split(jax.random.fold_in(key, 11), DEVICES)
    ticket = jnp.arange(PARENTS * CAPP, dtype=jnp.int32)
    ticket_parent = ticket // CAPP
    ticket_rank = ticket % CAPP
    parent_range = jnp.arange(PARENTS, dtype=jnp.int32)
    lowest = max(CAPP // 2, MINP)

    def one_device(worker_random_key):
        capped_random_key, order_key = jax.random.split(worker_random_key)
        row_ceiling = jax.random.randint(capped_random_key, (PARENTS,), lowest, CAPP + 1, dtype=jnp.int32)
        row_ceiling = jnp.where(parent_range == hot_parent, CAPP, row_ceiling)
        allowed = ticket_rank < row_ceiling[ticket_parent]
        forced = (ticket_rank < MINP) | (ticket_parent == hot_parent)
        priority = jax.random.randint(order_key, (PARENTS * CAPP,), 0, 1 << 20, dtype=jnp.int32)
        priority = jnp.where(forced, -1, jnp.where(allowed, priority, 1 << 21))
        picked = jnp.argsort(priority, stable=True)[:TOK_DEV].astype(jnp.int32)
        return (jnp.sort(picked) // CAPP).astype(jnp.int32)
    return jax.vmap(one_device)(device_keys).reshape(TOKENS)


def level_of(key, extent, cuts, least, largest):
    loudness, own = 1.0, jax.random.fold_in(key, 6)
    for position, shards_of in cuts:
        steps = jnp.exp(jax.random.uniform(jax.random.fold_in(own, position), (shards_of,), jnp.float32, least / len(cuts), largest / len(cuts)))
        loudness = loudness * jnp.repeat(steps, extent[position] // shards_of).reshape([-1 if axis == position else 1 for axis in range(len(extent))])
    return loudness


def centred(stream_key, extent, spread, limit, pieces=(), kind=jnp.bfloat16):
    result = jax.random.normal(stream_key, extent, jnp.float32) * spread
    if len(pieces) > 0:
        result = level_of(stream_key, extent, pieces, -0.22, 0.18) * result
    return jnp.clip(result, min=-limit, max=limit).astype(kind)


def setup_inputs(seed: int = 0) -> dict:
    streams_of = jax.random.split(jax.random.key(seed), 5)
    return {
        "embeddings": centred(streams_of[0], (TOKENS, D), 1.0, 6.0, ((0, 128),)),
        "embedding_parent_index": draw_embedding_parent_index(jax.random.fold_in(streams_of[4], 71), 0),
        "parent_slot": jax.random.permutation(streams_of[2], PARENTS).astype(jnp.int32),
        "centroids": centred(streams_of[3], (K, PARENTS, D), 1.0, 6.0, ((1, 16),)),
    }


softness_level = 0.1
prior_weight = 0.25

def unit_scale(values):
    return values * lax.rsqrt(lax.optimization_barrier(jnp.mean(values * values, axis=-1, keepdims=True)) + 1e-06)

def reference(embeddings, embedding_parent_index, parent_slot, centroids):
    width = centroids.shape[0]
    parent_count = centroids.shape[1]
    embedding_feature = centroids.shape[2]
    unit_children = unit_scale(centroids.astype(jnp.float32))
    low_children = unit_children.astype(jnp.bfloat16)
    ranked = jnp.argsort(embedding_parent_index, stable=True).astype(jnp.int32)
    sorted_ids = embedding_parent_index[ranked].astype(jnp.int32)
    block_rows = DEVICES
    shrink_multiplier = 1.0 / (softness_level * embedding_feature)

    def advance(child_total, step_index):
        begin_row = (step_index * block_rows).astype(jnp.int32)
        row_index = lax.dynamic_slice_in_dim(ranked, begin_row, block_rows)
        block_ids = lax.dynamic_slice_in_dim(sorted_ids, begin_row, block_rows)
        block_unit = unit_scale(embeddings[row_index].astype(jnp.float32)).astype(jnp.bfloat16)
        first_parent = block_ids[0]
        second_parent = jnp.minimum(first_parent + 1, parent_count - 1).astype(jnp.int32)
        slot_first = parent_slot[first_parent]
        slot_second = parent_slot[second_parent]
        candidates = jnp.concatenate([low_children[:, slot_first, :], low_children[:, slot_second, :]], axis=0)
        logits = jnp.dot(block_unit, candidates.T, preferred_element_type=jnp.float32) * shrink_multiplier
        in_first = (block_ids == first_parent)[:, None]
        chosen = jnp.where(in_first, logits[:, :width], logits[:, width:])
        weights = jax.nn.softmax(chosen, axis=-1).astype(jnp.bfloat16)
        nothing = jnp.zeros_like(weights)
        paired = jnp.concatenate([jnp.where(in_first, weights, nothing), jnp.where(in_first, nothing, weights)], axis=1)
        paired_sums = jnp.dot(paired.T, block_unit, preferred_element_type=jnp.float32)
        child_total = child_total.at[:, slot_first, :].add(paired_sums[:width])
        child_total = child_total.at[:, slot_second, :].add(paired_sums[width:])
        return (child_total, None)
    start_total = jnp.zeros((width, parent_count, embedding_feature), jnp.float32)
    steps_all = jnp.arange(TOKENS // block_rows, dtype=jnp.int32)
    child_total, _ = lax.scan(advance, start_total, steps_all)
    new_children = unit_scale(prior_weight * unit_children + child_total)
    new_parents = unit_scale(lax.optimization_barrier(jnp.sum(new_children, axis=0)))
    return (new_children, new_parents)
```

```python
import functools

import jax
import jax.numpy as jnp
from jax import lax
from jax.experimental import pallas as pl
from jax.experimental.pallas import tpu as pltpu
from jax.sharding import PartitionSpec as P

softness_level = 0.1
prior_weight = 0.25
EPS = 1e-06

CAP = 12
OWN = 4
ROWS = OWN * CAP
TILE = 16
GROUPS = ROWS // TILE
PAIRS = 4
WIN = 32


def unit_scale(values):
    return values * lax.rsqrt(jnp.mean(values * values, axis=-1, keepdims=True) + EPS)


def pack_kernel(outers, owned, start_ref, count_ref, rows_ref, out_ref, unit_ref):
    total, width = rows_ref.shape
    step = pl.program_id(0)
    chunk = 64

    @pl.when(step == 0)
    def _():
        unit_ref[total:, :] = jnp.zeros((unit_ref.shape[0] - total, width), jnp.bfloat16)

        def normalise(i, carry):
            at = pl.ds(pl.multiple_of(i * chunk, chunk), chunk)
            unit_ref[at, :] = unit_scale(rows_ref[at, :].astype(jnp.float32)).astype(jnp.bfloat16)
            return carry

        lax.fori_loop(0, total // chunk, normalise, 0, unroll=4)

    row = lax.broadcasted_iota(jnp.int32, (2 * ROWS, 1), 0)
    half = (row >= ROWS).astype(jnp.int32)
    inner = row - half * ROWS
    group = lax.shift_right_logical(inner, 4)
    place = inner & (TILE - 1)
    first = place < CAP
    source = half * OWN + jnp.where(first, group, OWN - 1)
    position = jnp.where(first, place, group * (TILE - CAP) + place - CAP)
    column = lax.broadcasted_iota(jnp.int32, (2 * ROWS, 2 * OWN * WIN), 1)
    for pair in range(PAIRS):
        target = jnp.full((2 * ROWS, 1), -1, jnp.int32)
        windows = []
        for q in range(2 * OWN):
            device = (step * PAIRS + pair) * 2 + q // OWN
            slot = lax.rem(device, outers) * owned + lax.div(device, outers) * OWN + q % OWN
            start = start_ref[slot]
            count = count_ref[slot]
            aligned = lax.shift_left(lax.shift_right_logical(start, 4), 4)
            windows.append(unit_ref[pl.ds(pl.multiple_of(aligned, TILE), WIN), :])
            spot = q * WIN + (start - aligned) + position
            target = jnp.where((source == q) & (position < count), spot, target)
        selector = (column == target).astype(jnp.float32).astype(jnp.bfloat16)
        window = jnp.concatenate(windows, axis=0)
        out_ref[pair * 2 * ROWS : (pair + 1) * 2 * ROWS, :] = jnp.dot(
            selector, window, preferred_element_type=jnp.float32
        ).astype(jnp.bfloat16)


def pack(embeddings, starts, counts, outers, owned, devices):
    total, width = embeddings.shape
    return pl.pallas_call(
        functools.partial(pack_kernel, outers, owned),
        out_shape=jax.ShapeDtypeStruct((devices * ROWS, width), jnp.bfloat16),
        grid_spec=pltpu.PrefetchScalarGridSpec(
            num_scalar_prefetch=2,
            grid=(devices // (2 * PAIRS),),
            in_specs=[
                pl.BlockSpec((total, width), lambda i, s, c: (0, 0), pipeline_mode=pl.Buffered(1))
            ],
            out_specs=pl.BlockSpec((2 * ROWS * PAIRS, width), lambda i, s, c: (i, 0)),
            scratch_shapes=[pltpu.VMEM((total + WIN, width), jnp.bfloat16)],
        ),
        compiler_params=pltpu.CompilerParams(vmem_limit_bytes=40 << 20),
        name="pack",
    )(starts, counts, embeddings)


def sums_kernel(shrink, per_node, rows_ref, low_ref, unit_ref, out_ref, total_ref):
    step = pl.program_id(0)
    block, width = rows_ref.shape
    sources = block // ROWS
    children = low_ref.shape[1]

    @pl.when(step == 0)
    def _():
        total_ref[...] = jnp.zeros_like(total_ref)

    lane = lax.broadcasted_iota(jnp.int32, (1, sources * TILE), 1)
    first = (lane & (TILE - 1)) < CAP
    for g in range(GROUPS):
        rows = jnp.concatenate(
            [rows_ref[b * ROWS + g * TILE : b * ROWS + (g + 1) * TILE, :] for b in range(sources)],
            axis=0,
        )
        low = jnp.concatenate([low_ref[g], low_ref[OWN - 1]], axis=0)
        logits = lax.dot_general(
            low, rows, (((1,), (1,)), ((), ())), preferred_element_type=jnp.float32
        )
        chosen = jnp.where(first, logits[:children], logits[children:]) * shrink
        raised = jnp.exp(chosen)
        weights = raised / jnp.sum(raised, axis=0, keepdims=True)
        zero = jnp.zeros_like(weights)
        paired = jnp.concatenate(
            [jnp.where(first, weights, zero), jnp.where(first, zero, weights)], axis=0
        ).astype(jnp.bfloat16)
        sums = jnp.dot(paired, rows, preferred_element_type=jnp.float32)
        total_ref[g] += sums[:children]
        total_ref[OWN - 1] += sums[children:]

    @pl.when(step == pl.num_programs(0) - 1)
    def _():
        parents = []
        for j in range(OWN):
            fresh = unit_scale(prior_weight * unit_ref[j] + total_ref[j])
            parents.append(unit_scale(jnp.sum(fresh, axis=0, keepdims=True)))
            fresh = fresh.astype(jnp.bfloat16)
            for m in range(children // per_node):
                out_ref[m, j * per_node : (j + 1) * per_node, :] = fresh[
                    m * per_node : (m + 1) * per_node
                ]
        tail = jnp.concatenate(parents + parents, axis=0).astype(jnp.bfloat16)
        for m in range(children // per_node):
            out_ref[m, OWN * per_node :, :] = tail


def child_sums(arrived, low, unit, shrink, nodes):
    total, width = arrived.shape
    children = low.shape[1]
    per_node = children // nodes
    block = 32 * ROWS
    whole = lambda i: (0, 0, 0)
    return pl.pallas_call(
        functools.partial(sums_kernel, shrink, per_node),
        out_shape=jax.ShapeDtypeStruct((nodes, OWN * per_node + 2 * OWN, width), jnp.bfloat16),
        grid=(total // block,),
        in_specs=[
            pl.BlockSpec((block, width), lambda i: (i, 0)),
            pl.BlockSpec(low.shape, whole, pipeline_mode=pl.Buffered(1)),
            pl.BlockSpec(unit.shape, whole, pipeline_mode=pl.Buffered(1)),
        ],
        out_specs=pl.BlockSpec((nodes, OWN * per_node + 2 * OWN, width), whole),
        scratch_shapes=[pltpu.VMEM((OWN, children, width), jnp.float32)],
        compiler_params=pltpu.CompilerParams(vmem_limit_bytes=48 << 20),
        name="child_sums",
    )(arrived, low, unit)


def order_kernel(per_node, rows_ref, children_ref, parents_ref):
    block = OWN * per_node + 2 * OWN
    nodes = rows_ref.shape[0] // block
    slots = nodes * OWN
    column = lax.broadcasted_iota(jnp.int32, (1, rows_ref.shape[0]), 1)
    out = lax.broadcasted_iota(jnp.int32, (per_node * slots, 1), 0)
    slot = out & (slots - 1)
    child = lax.div(out, slots)
    wanted = lax.div(slot, OWN) * block + (slot & (OWN - 1)) * per_node + child
    mover = (wanted == column).astype(jnp.float32).astype(jnp.bfloat16)
    rows = rows_ref[...]
    children_ref[...] = jnp.dot(mover, rows, preferred_element_type=jnp.float32)
    slot = lax.broadcasted_iota(jnp.int32, (slots, 1), 0)
    wanted = lax.div(slot, OWN) * block + OWN * per_node + (slot & (OWN - 1))
    mover = (wanted == column).astype(jnp.float32).astype(jnp.bfloat16)
    parents_ref[...] = jnp.dot(mover, rows, preferred_element_type=jnp.float32)


def put_in_order(received, per_node):
    nodes, block, width = received.shape
    slots = nodes * OWN
    children, parents = pl.pallas_call(
        functools.partial(order_kernel, per_node),
        out_shape=(
            jax.ShapeDtypeStruct((per_node * slots, width), jnp.float32),
            jax.ShapeDtypeStruct((slots, width), jnp.float32),
        ),
        name="put_in_order",
    )(received.reshape(nodes * block, width))
    return children.reshape(per_node, slots, width), parents


def body(embeddings, embedding_parent_index, parent_slot, centroids):
    width = embeddings.shape[1]
    children, owned, _ = centroids.shape
    parent_count = parent_slot.shape[0]
    nodes = lax.axis_size("node")
    outers = lax.axis_size("outer")
    devices = nodes * outers
    shrink = 1.0 / (softness_level * width)
    node = lax.axis_index("node")

    ids = jnp.arange(parent_count, dtype=jnp.int32)
    held = (parent_slot[None, :] == ids[:, None]).astype(jnp.int32)
    parent_of_slot = jnp.sum(held * ids[None, :], axis=1)
    starts = jnp.sum(
        (embedding_parent_index[None, :] < parent_of_slot[:, None]).astype(jnp.int32), axis=1
    )
    counts = jnp.sum(
        (embedding_parent_index[None, :] == parent_of_slot[:, None]).astype(jnp.int32), axis=1
    )
    own = lax.dynamic_slice_in_dim(centroids, node * OWN, OWN, 1).transpose(1, 0, 2)
    unit = unit_scale(own.astype(jnp.float32))
    low = unit.astype(jnp.bfloat16)
    packed = pack(embeddings, starts, counts, outers, owned, devices)
    packed, unit, low = lax.optimization_barrier((packed, unit, low))
    arrived = lax.all_to_all(
        packed.reshape(devices, ROWS, width),
        ("node", "outer"),
        split_axis=0,
        concat_axis=0,
        tiled=True,
    )
    fresh = child_sums(
        arrived.reshape(devices * ROWS, width), low, unit, shrink, nodes
    )
    received = lax.all_to_all(fresh, "node", split_axis=0, concat_axis=0, tiled=True)
    return put_in_order(received, children // nodes)


def solution(mesh):
    placed = (P(("node", "outer"), None), P(("node", "outer")), P(), P(None, "outer", None))
    return jax.shard_map(
        body,
        mesh=mesh,
        in_specs=placed,
        out_specs=(P("node", "outer", None), P("outer", None)),
        check_vma=False,
    )
```

```python
import functools

import jax
import jax.numpy as jnp
from jax import lax
from jax.experimental import pallas as pl
from jax.experimental.pallas import tpu as pltpu
from jax.sharding import PartitionSpec as P

softness_level = 0.1
prior_weight = 0.25
EPS = 1e-06

CAP = 12
OWN = 4
ROWS = OWN * CAP
TILE = 16
GROUPS = ROWS // TILE
PAIRS = 4
WIN = 32
SHORT = 32
GUESTS = 2
DENSE_PAIRS = 4
LANES = 128
NOBODY = 64


def unit_scale(values):
    return values * lax.rsqrt(jnp.mean(values * values, axis=-1, keepdims=True) + EPS)


def pack_kernel(outers, owned, start_ref, count_ref, rows_ref, out_ref, unit_ref):
    total, width = rows_ref.shape
    step = pl.program_id(0)
    chunk = 64

    @pl.when(step == 0)
    def _():
        unit_ref[total:, :] = jnp.zeros((unit_ref.shape[0] - total, width), jnp.bfloat16)

        def normalise(i, carry):
            at = pl.ds(pl.multiple_of(i * chunk, chunk), chunk)
            unit_ref[at, :] = unit_scale(rows_ref[at, :].astype(jnp.float32)).astype(jnp.bfloat16)
            return carry

        lax.fori_loop(0, total // chunk, normalise, 0, unroll=4)

    row = lax.broadcasted_iota(jnp.int32, (2 * ROWS, 1), 0)
    half = (row >= ROWS).astype(jnp.int32)
    inner = row - half * ROWS
    group = lax.shift_right_logical(inner, 4)
    place = inner & (TILE - 1)
    first = place < CAP
    source = half * OWN + jnp.where(first, group, OWN - 1)
    position = jnp.where(first, place, group * (TILE - CAP) + place - CAP)
    column = lax.broadcasted_iota(jnp.int32, (2 * ROWS, 2 * OWN * WIN), 1)
    for pair in range(PAIRS):
        target = jnp.full((2 * ROWS, 1), -1, jnp.int32)
        windows = []
        for q in range(2 * OWN):
            device = (step * PAIRS + pair) * 2 + q // OWN
            slot = lax.rem(device, outers) * owned + lax.div(device, outers) * OWN + q % OWN
            start = start_ref[slot]
            count = count_ref[slot]
            aligned = lax.shift_left(lax.shift_right_logical(start, 4), 4)
            windows.append(unit_ref[pl.ds(pl.multiple_of(aligned, TILE), WIN), :])
            spot = q * WIN + (start - aligned) + position
            target = jnp.where((source == q) & (position < count), spot, target)
        selector = (column == target).astype(jnp.float32).astype(jnp.bfloat16)
        window = jnp.concatenate(windows, axis=0)
        out_ref[pair * 2 * ROWS : (pair + 1) * 2 * ROWS, :] = jnp.dot(
            selector, window, preferred_element_type=jnp.float32
        ).astype(jnp.bfloat16)


def pack(embeddings, starts, counts, outers, owned, devices):
    total, width = embeddings.shape
    return pl.pallas_call(
        functools.partial(pack_kernel, outers, owned),
        out_shape=jax.ShapeDtypeStruct((devices * ROWS, width), jnp.bfloat16),
        grid_spec=pltpu.PrefetchScalarGridSpec(
            num_scalar_prefetch=2,
            grid=(devices // (2 * PAIRS),),
            in_specs=[
                pl.BlockSpec((total, width), lambda i, s, c: (0, 0), pipeline_mode=pl.Buffered(1))
            ],
            out_specs=pl.BlockSpec((2 * ROWS * PAIRS, width), lambda i, s, c: (i, 0)),
            scratch_shapes=[pltpu.VMEM((total + WIN, width), jnp.bfloat16)],
        ),
        compiler_params=pltpu.CompilerParams(vmem_limit_bytes=40 << 20),
        name="pack",
    )(starts, counts, embeddings)


def sums_kernel(shrink, per_node, rows_ref, low_ref, unit_ref, out_ref, total_ref):
    step = pl.program_id(0)
    block, width = rows_ref.shape
    sources = block // ROWS
    children = low_ref.shape[1]

    @pl.when(step == 0)
    def _():
        total_ref[...] = jnp.zeros_like(total_ref)

    lane = lax.broadcasted_iota(jnp.int32, (1, sources * TILE), 1)
    first = (lane & (TILE - 1)) < CAP
    for g in range(GROUPS):
        rows = jnp.concatenate(
            [rows_ref[b * ROWS + g * TILE : b * ROWS + (g + 1) * TILE, :] for b in range(sources)],
            axis=0,
        )
        low = jnp.concatenate([low_ref[g], low_ref[OWN - 1]], axis=0)
        logits = lax.dot_general(
            low, rows, (((1,), (1,)), ((), ())), preferred_element_type=jnp.float32
        )
        chosen = jnp.where(first, logits[:children], logits[children:]) * shrink
        raised = jnp.exp(chosen)
        weights = raised / jnp.sum(raised, axis=0, keepdims=True)
        zero = jnp.zeros_like(weights)
        paired = jnp.concatenate(
            [jnp.where(first, weights, zero), jnp.where(first, zero, weights)], axis=0
        ).astype(jnp.bfloat16)
        sums = jnp.dot(paired, rows, preferred_element_type=jnp.float32)
        total_ref[g] += sums[:children]
        total_ref[OWN - 1] += sums[children:]

    @pl.when(step == pl.num_programs(0) - 1)
    def _():
        parents = []
        for j in range(OWN):
            fresh = unit_scale(prior_weight * unit_ref[j] + total_ref[j])
            parents.append(unit_scale(jnp.sum(fresh, axis=0, keepdims=True)))
            fresh = fresh.astype(jnp.bfloat16)
            for m in range(children // per_node):
                out_ref[m, j * per_node : (j + 1) * per_node, :] = fresh[
                    m * per_node : (m + 1) * per_node
                ]
        tail = jnp.concatenate(parents + parents, axis=0).astype(jnp.bfloat16)
        for m in range(children // per_node):
            out_ref[m, OWN * per_node :, :] = tail


def child_sums(arrived, low, unit, shrink, nodes):
    total, width = arrived.shape
    children = low.shape[1]
    per_node = children // nodes
    block = 32 * ROWS
    whole = lambda i: (0, 0, 0)
    return pl.pallas_call(
        functools.partial(sums_kernel, shrink, per_node),
        out_shape=jax.ShapeDtypeStruct((nodes, OWN * per_node + 2 * OWN, width), jnp.bfloat16),
        grid=(total // block,),
        in_specs=[
            pl.BlockSpec((block, width), lambda i: (i, 0)),
            pl.BlockSpec(low.shape, whole, pipeline_mode=pl.Buffered(1)),
            pl.BlockSpec(unit.shape, whole, pipeline_mode=pl.Buffered(1)),
        ],
        out_specs=pl.BlockSpec((nodes, OWN * per_node + 2 * OWN, width), whole),
        scratch_shapes=[pltpu.VMEM((OWN, children, width), jnp.float32)],
        compiler_params=pltpu.CompilerParams(vmem_limit_bytes=48 << 20),
        name="child_sums",
    )(arrived, low, unit)


def order_kernel(per_node, rows_ref, children_ref, parents_ref):
    block = OWN * per_node + 2 * OWN
    nodes = rows_ref.shape[0] // block
    slots = nodes * OWN
    column = lax.broadcasted_iota(jnp.int32, (1, rows_ref.shape[0]), 1)
    out = lax.broadcasted_iota(jnp.int32, (per_node * slots, 1), 0)
    slot = out & (slots - 1)
    child = lax.div(out, slots)
    wanted = lax.div(slot, OWN) * block + (slot & (OWN - 1)) * per_node + child
    mover = (wanted == column).astype(jnp.float32).astype(jnp.bfloat16)
    rows = rows_ref[...]
    children_ref[...] = jnp.dot(mover, rows, preferred_element_type=jnp.float32)
    slot = lax.broadcasted_iota(jnp.int32, (slots, 1), 0)
    wanted = lax.div(slot, OWN) * block + OWN * per_node + (slot & (OWN - 1))
    mover = (wanted == column).astype(jnp.float32).astype(jnp.bfloat16)
    parents_ref[...] = jnp.dot(mover, rows, preferred_element_type=jnp.float32)


def put_in_order(received, per_node):
    nodes, block, width = received.shape
    slots = nodes * OWN
    children, parents = pl.pallas_call(
        functools.partial(order_kernel, per_node),
        out_shape=(
            jax.ShapeDtypeStruct((per_node * slots, width), jnp.float32),
            jax.ShapeDtypeStruct((slots, width), jnp.float32),
        ),
        name="put_in_order",
    )(received.reshape(nodes * block, width))
    return children.reshape(per_node, slots, width), parents


def dense_pack_kernel(
    outers,
    owned,
    plan_ref,
    spill_ref,
    rows_ref,
    common_ref,
    out_ref,
    unit_ref,
):
    total, width = rows_ref.shape
    step = pl.program_id(0)
    chunk = 64

    @pl.when(step == 0)
    def _():
        unit_ref[total:, :] = jnp.zeros((unit_ref.shape[0] - total, width), jnp.bfloat16)

        def normalise(i, carry):
            at = pl.ds(pl.multiple_of(i * chunk, chunk), chunk)
            unit_ref[at, :] = unit_scale(rows_ref[at, :].astype(jnp.float32)).astype(jnp.bfloat16)
            return carry

        lax.fori_loop(0, total // chunk, normalise, 0, unroll=4)

    row = lax.broadcasted_iota(jnp.int32, (2 * SHORT, 1), 0)
    half = lax.shift_right_logical(row, 5)
    place = (row & (SHORT - 1)) - 1
    column = lax.broadcasted_iota(jnp.int32, (2 * SHORT, 2 * OWN * WIN), 1)
    lane = lax.broadcasted_iota(jnp.int32, (1, LANES), 1)
    lane_place = (lane & (SHORT - 1)) - 1
    top = lax.broadcasted_iota(jnp.int32, (8, 1), 0) == 0
    blank = jnp.zeros((1, LANES), jnp.float32)
    filler = jnp.zeros((1, width - 3 * LANES), jnp.float32)
    for pair in range(DENSE_PAIRS):
        target = jnp.full((2 * SHORT, 1), -1, jnp.int32)
        windows = []
        heads = []
        for h in range(2):
            device = (step * DENSE_PAIRS + pair) * 2 + h
            base = lax.rem(device, outers) * owned + lax.div(device, outers) * OWN
            low_end = jnp.int32(0)
            slots = jnp.full((1, LANES), NOBODY, jnp.int32)
            for j in range(OWN):
                start = plan_ref[0, base + j]
                high_end = jnp.minimum(low_end + plan_ref[1, base + j], SHORT - 1)
                aligned = lax.shift_left(lax.shift_right_logical(start, 4), 4)
                windows.append(unit_ref[pl.ds(pl.multiple_of(aligned, TILE), WIN), :])
                spot = (h * OWN + j) * WIN + (start - aligned) - low_end + place
                target = jnp.where(
                    (half == h) & (place >= low_end) & (place < high_end), spot, target
                )
                slots = jnp.where((lane_place >= low_end) & (lane_place < high_end), j, slots)
                low_end = high_end
            heads.append(
                jnp.concatenate(
                    [slots.astype(jnp.float32), common_ref[0:1, :], common_ref[1:2, :], filler],
                    axis=1,
                )
            )
        selector = (column == target).astype(jnp.float32).astype(jnp.bfloat16)
        moved = jnp.dot(
            selector, jnp.concatenate(windows, axis=0), preferred_element_type=jnp.float32
        )
        pieces = []
        for h in range(2):
            pieces.append(jnp.where(top, heads[h], moved[h * SHORT : h * SHORT + 8]))
            pieces.append(moved[h * SHORT + 8 : (h + 1) * SHORT])
        out_ref[pair * 2 * SHORT : (pair + 1) * 2 * SHORT, :] = jnp.concatenate(
            pieces, axis=0
        ).astype(jnp.bfloat16)

    tile_row = lax.broadcasted_iota(jnp.int32, (TILE, 1), 0)
    for m in range(2 * DENSE_PAIRS):
        device = step * 2 * DENSE_PAIRS + m
        outer = lax.rem(device, outers)
        base = outer * owned + lax.div(device, outers) * OWN
        guests = plan_ref[2, base]
        for i in range(GUESTS):

            @pl.when(guests > i)
            def _():
                entry = plan_ref[3, base] + i * plan_ref[4, base]
                source = spill_ref[outer, entry]
                slot = spill_ref[outers + outer, entry].astype(jnp.float32)
                aligned = lax.shift_left(lax.shift_right_logical(source, 4), 4)
                tile = unit_ref[pl.ds(pl.multiple_of(aligned, TILE), TILE), :].astype(jnp.float32)
                chosen = jnp.sum(
                    jnp.where(tile_row == source - aligned, tile, 0.0), axis=0, keepdims=True
                )
                tail = slice(m * SHORT + TILE, (m + 1) * SHORT)
                kept = out_ref[tail, :].astype(jnp.float32)
                out_ref[tail, :] = jnp.where(tile_row == TILE - 1 - i, chosen, kept).astype(
                    jnp.bfloat16
                )
                head = slice(m * SHORT, m * SHORT + TILE)
                where = slice(3 * LANES, 4 * LANES)
                kept = out_ref[head, where].astype(jnp.float32)
                mine = (tile_row == 0) & ((lane & 7) == 7 - i)
                out_ref[head, where] = jnp.where(mine, slot, kept).astype(jnp.bfloat16)


def dense_pack(embeddings, scalars, common, outers, owned, devices):
    total, width = embeddings.shape
    block = 2 * SHORT * DENSE_PAIRS
    return pl.pallas_call(
        functools.partial(dense_pack_kernel, outers, owned),
        out_shape=jax.ShapeDtypeStruct((devices * SHORT, width), jnp.bfloat16),
        grid_spec=pltpu.PrefetchScalarGridSpec(
            num_scalar_prefetch=len(scalars),
            grid=(devices // (2 * DENSE_PAIRS),),
            in_specs=[
                pl.BlockSpec((total, width), lambda i, *_: (0, 0), pipeline_mode=pl.Buffered(1)),
                pl.BlockSpec((2, LANES), lambda i, *_: (0, 0), pipeline_mode=pl.Buffered(1)),
            ],
            out_specs=pl.BlockSpec((block, width), lambda i, *_: (i, 0)),
            scratch_shapes=[pltpu.VMEM((total + WIN, width), jnp.bfloat16)],
        ),
        compiler_params=pltpu.CompilerParams(vmem_limit_bytes=54 << 20),
        name="dense_pack",
    )(*scalars, embeddings, common)


def collect_kernel(me_ref, rows_ref, head_ref, late_ref, notes_ref, unfit_ref, wide_ref):
    sources = rows_ref.shape[0]
    width = rows_ref.shape[2]
    columns = sources * 8
    heads = head_ref[...].astype(jnp.float32).reshape(sources * 8, head_ref.shape[2])
    notes = []
    for q in range(wide_ref.shape[0]):
        wide_ref[q] = heads[:, q * LANES : (q + 1) * LANES]
        notes.append(wide_ref[q, pl.ds(0, sources, stride=8), :])
    notes = jnp.concatenate(notes, axis=1)
    notes_ref[...] = notes[:, :LANES]
    everyone = notes[:, LANES : 2 * LANES]
    crowded = jnp.max(jnp.sum(everyone, axis=0, keepdims=True)) > SHORT - 1
    failed = jnp.max(notes[:, 2 * LANES : 3 * LANES]) > 0.0
    unfit_ref[0] = (crowded | failed).astype(jnp.int32)

    lane = lax.broadcasted_iota(jnp.int32, (1, LANES), 1)
    guests = jnp.sum(jnp.where(lane == me_ref[0], everyone, 0.0), axis=1, keepdims=True)
    column = lax.broadcasted_iota(jnp.int32, (1, columns), 1)
    owner = lax.shift_right_logical(column, 3)
    source = lax.broadcasted_iota(jnp.int32, (sources, 1), 0)
    before = jnp.sum(jnp.where(source < owner, guests, 0.0), axis=0, keepdims=True)
    here = jnp.sum(jnp.where(source == owner, guests, 0.0), axis=0, keepdims=True)
    slots = jnp.concatenate([notes[:, 3 * LANES :]] * (columns // LANES), axis=1)
    slots = jnp.sum(jnp.where(source == owner, slots, 0.0), axis=0, keepdims=True)
    order = 7 - (column & 7)
    place = jnp.where(order < here.astype(jnp.int32), before.astype(jnp.int32) + order + 1, -1)
    wanted = lax.broadcasted_iota(jnp.int32, (LANES, 1), 0) & (SHORT - 1)
    selector = (wanted == place).astype(jnp.float32).astype(jnp.bfloat16)
    slots = jnp.broadcast_to(slots, (8, columns)).astype(jnp.bfloat16)
    head = lax.dot_general(
        slots, selector, (((1,), (1,)), ((), ())), preferred_element_type=jnp.float32
    )[0:1]
    head = jnp.concatenate([head] * (width // LANES), axis=1)
    rows = rows_ref[...].astype(jnp.float32).reshape(columns, width).astype(jnp.bfloat16)
    moved = jnp.dot(selector[:SHORT], rows, preferred_element_type=jnp.float32)
    top = lax.broadcasted_iota(jnp.int32, (SHORT, 1), 0) == 0
    moved = jnp.where(top, head, moved).astype(jnp.bfloat16)
    for n in range(late_ref.shape[0]):
        late_ref[n] = moved


def collect(arrived, me, nodes):
    sources, short, width = arrived.shape
    return pl.pallas_call(
        collect_kernel,
        out_shape=(
            jax.ShapeDtypeStruct((nodes, SHORT, width), jnp.bfloat16),
            jax.ShapeDtypeStruct((sources, LANES), jnp.float32),
            jax.ShapeDtypeStruct((1,), jnp.int32),
        ),
        grid_spec=pltpu.PrefetchScalarGridSpec(
            num_scalar_prefetch=1,
            grid=(1,),
            in_specs=[
                pl.BlockSpec((sources, 8, width), lambda i, m: (0, short // 8 - 1, 0)),
                pl.BlockSpec((sources, 8, 4 * LANES), lambda i, m: (0, 0, 0)),
            ],
            out_specs=(
                pl.BlockSpec((nodes, SHORT, width), lambda i, m: (0, 0, 0)),
                pl.BlockSpec((sources, LANES), lambda i, m: (0, 0)),
                pl.BlockSpec(memory_space=pltpu.SMEM),
            ),
            scratch_shapes=[pltpu.VMEM((4, sources * 8, LANES), jnp.float32)],
        ),
        compiler_params=pltpu.CompilerParams(vmem_limit_bytes=58 << 20),
        name="collect",
    )(me, arrived, arrived)


def weighted_rows(low, rows, slots, shrink):
    children = low.shape[0] // OWN
    logits = lax.dot_general(
        low, rows, (((1,), (1,)), ((), ())), preferred_element_type=jnp.float32
    )
    chosen = jnp.zeros((children, rows.shape[0]), jnp.float32)
    for j in range(OWN):
        chosen = jnp.where(slots == j, logits[j * children : (j + 1) * children], chosen)
    raised = jnp.exp(chosen * shrink)
    weights = raised / jnp.sum(raised, axis=0, keepdims=True)
    spread = jnp.concatenate(
        [jnp.where(slots == j, weights, 0.0) for j in range(OWN)], axis=0
    ).astype(jnp.bfloat16)
    return jnp.dot(spread, rows, preferred_element_type=jnp.float32)


def along_lanes(notes):
    count = notes.shape[0]
    column = lax.broadcasted_iota(jnp.int32, (1, count * SHORT), 1)
    source = lax.broadcasted_iota(jnp.int32, (count, 1), 0)
    wide = jnp.concatenate([notes] * (count * SHORT // LANES), axis=1)
    mine = source == lax.shift_right_logical(column, 5)
    return jnp.sum(jnp.where(mine, wide, 0.0), axis=0, keepdims=True).astype(jnp.int32)


def dense_sums_kernel(shrink, rows_ref, notes_ref, low_ref, total_ref):
    sums = weighted_rows(low_ref[...], rows_ref[...], along_lanes(notes_ref[...]), shrink)

    @pl.when(pl.program_id(0) == 0)
    def _():
        total_ref[...] = sums

    @pl.when(pl.program_id(0) > 0)
    def _():
        total_ref[...] += sums


def dense_sums(arrived, notes, low, shrink):
    total, width = arrived.shape
    block = 32 * SHORT
    return pl.pallas_call(
        functools.partial(dense_sums_kernel, shrink),
        out_shape=jax.ShapeDtypeStruct(low.shape, jnp.float32),
        grid=(total // block,),
        in_specs=[
            pl.BlockSpec((block, width), lambda i: (i, 0)),
            pl.BlockSpec((block // SHORT, LANES), lambda i: (i, 0)),
            pl.BlockSpec(low.shape, lambda i: (0, 0), pipeline_mode=pl.Buffered(1)),
        ],
        out_specs=pl.BlockSpec(low.shape, lambda i: (0, 0)),
        compiler_params=pltpu.CompilerParams(vmem_limit_bytes=48 << 20),
        cost_estimate=pl.CostEstimate(
            flops=4 * total * width * low.shape[0],
            bytes_accessed=2 * total * width + 6 * low.size,
            transcendentals=total * low.shape[0] // OWN,
        ),
        name="dense_sums",
    )(arrived, notes, low)


def finish_kernel(shrink, per_node, node_ref, total_ref, late_ref, low_ref, unit_ref, out_ref):
    children = unit_ref.shape[1]
    late = late_ref.shape[0] // SHORT
    notes = jnp.concatenate(
        [
            late_ref[b * SHORT : b * SHORT + TILE, :LANES].astype(jnp.float32)[0:1]
            for b in range(late)
        ],
        axis=0,
    )
    slots = along_lanes(notes) - 1 - OWN * node_ref[0]
    added = weighted_rows(low_ref[...], late_ref[...], slots, shrink)
    parents = []
    for j in range(OWN):
        at = slice(j * children, (j + 1) * children)
        fresh = unit_scale(prior_weight * unit_ref[j] + (total_ref[at, :] + added[at]))
        parents.append(unit_scale(jnp.sum(fresh, axis=0, keepdims=True)))
        fresh = fresh.astype(jnp.bfloat16)
        for m in range(children // per_node):
            out_ref[m, j * per_node : (j + 1) * per_node, :] = fresh[
                m * per_node : (m + 1) * per_node
            ]
    tail = jnp.concatenate(parents + parents, axis=0).astype(jnp.bfloat16)
    for m in range(children // per_node):
        out_ref[m, OWN * per_node :, :] = tail


def finish(total, late, low, unit, node, shrink, nodes):
    per_node = unit.shape[1] // nodes
    out = (nodes, OWN * per_node + 2 * OWN, late.shape[1])
    return pl.pallas_call(
        functools.partial(finish_kernel, shrink, per_node),
        out_shape=jax.ShapeDtypeStruct(out, jnp.bfloat16),
        in_specs=[pl.BlockSpec(memory_space=pltpu.SMEM)]
        + [pl.BlockSpec(memory_space=pltpu.VMEM)] * 4,
        compiler_params=pltpu.CompilerParams(vmem_limit_bytes=48 << 20),
        name="finish",
    )(node, total, late, low, unit)


def plan_kernel(outers, nodes, rank_ref, slot_ref, ids_ref, plan_ref, spill_ref, common_ref):
    slots = slot_ref.shape[1]
    owned = slots // outers
    room = SHORT - 1
    row = lax.broadcasted_iota(jnp.int32, (slots, 1), 0)
    other = lax.broadcasted_iota(jnp.int32, (1, slots), 1)
    lane = lax.broadcasted_iota(jnp.int32, (1, LANES), 1)
    parent = jnp.sum(
        jnp.where(slot_ref[...] == row, other.astype(jnp.float32), 0.0), axis=1, keepdims=True
    ).astype(jnp.int32)
    ids = ids_ref[...]
    starts = []
    counts = []
    for at in range(0, slots, 64):
        mine = parent[at : at + 64]
        below = jnp.where(ids < mine, 1.0, 0.0)
        equal = jnp.where(ids == mine, 1.0, 0.0)
        starts.append(jnp.sum(below, axis=1, keepdims=True))
        counts.append(jnp.sum(equal, axis=1, keepdims=True))
    starts = jnp.concatenate(starts, axis=0)
    counts = jnp.concatenate(counts, axis=0)

    def total(mask, columns):
        wide = jnp.zeros((slots, LANES), jnp.float32)
        for q, value in enumerate(columns):
            wide = jnp.where(lane == q, value, wide)
        mask = mask.astype(jnp.float32).astype(jnp.bfloat16)
        sums = jnp.dot(mask, wide.astype(jnp.bfloat16), preferred_element_type=jnp.float32)
        return [sums[:, q : q + 1] for q in range(len(columns))]

    group = lax.shift_right_logical(row, 2)
    other_group = lax.shift_right_logical(other, 2)
    outer = lax.div(row, owned)
    other_outer = lax.div(other, owned)
    (first,) = total((group == other_group) & (other < row), [counts])
    (sent,) = total(group == other_group, [counts])
    over = jnp.maximum(sent - room, 0.0)
    host = jnp.where(sent <= room - GUESTS, 1.0, 0.0)
    once = jnp.where((row & (OWN - 1)) == 0, 1.0, 0.0)
    parts = [over * once, host * once]
    over_first, host_first = total((outer == other_outer) & (other_group < group), parts)
    overs, real_hosts = total(outer == other_outer, parts)
    hosts = jnp.maximum(real_hosts, 1.0)
    shift = jnp.zeros_like(hosts)
    for h in range(1, nodes + 1):
        shift = jnp.where(hosts == h, lax.rem(rank_ref[0], h).astype(jnp.float32), shift)
    turn = host_first - shift
    turn = jnp.where(turn < 0.0, turn + hosts, turn)
    guests = host * (
        jnp.where(overs > turn, 1.0, 0.0) + jnp.where(overs > turn + hosts, 1.0, 0.0)
    )
    failed = jnp.max(overs - GUESTS * real_hosts) > 0.0

    wide = jnp.zeros((slots, LANES), jnp.float32)
    for q, value in enumerate([starts, counts, guests, turn, hosts]):
        wide = jnp.where(lane == q, value, wide)
    plan_ref[...] = jnp.transpose(wide)[:8].astype(jnp.int32)

    begin = over_first + jnp.maximum(first - room, 0.0)
    end = over_first + jnp.maximum(first + counts - room, 0.0)
    entry = lane.astype(jnp.float32)
    held = (begin <= entry) & (entry < end)
    source = jnp.where(held, starts - first + room - over_first + entry, 0.0)
    named = jnp.where(held, ((row & (owned - 1)) + 1).astype(jnp.float32), 0.0)
    for o in range(outers):
        at = slice(o * owned, (o + 1) * owned)
        spill_ref[o : o + 1, :] = jnp.sum(source[at], axis=0, keepdims=True).astype(jnp.int32)
        spill_ref[outers + o : outers + o + 1, :] = jnp.sum(
            named[at], axis=0, keepdims=True
        ).astype(jnp.int32)
    where = (lane & (outers - 1)) * owned + lax.div(lane, outers) * OWN
    common_ref[0:1, :] = jnp.sum(jnp.where(row == where, guests, 0.0), axis=0, keepdims=True)
    common_ref[1:2, :] = jnp.broadcast_to(failed.astype(jnp.float32), (1, LANES))


def plan(parent_slot, embedding_parent_index, rank, outers, nodes):
    slots = parent_slot.shape[0]
    return pl.pallas_call(
        functools.partial(plan_kernel, outers, nodes),
        out_shape=(
            jax.ShapeDtypeStruct((8, slots), jnp.int32),
            jax.ShapeDtypeStruct((2 * outers, LANES), jnp.int32),
            jax.ShapeDtypeStruct((2, LANES), jnp.float32),
        ),
        in_specs=[pl.BlockSpec(memory_space=pltpu.SMEM)]
        + [pl.BlockSpec(memory_space=pltpu.VMEM)] * 2,
        name="plan",
    )(rank, parent_slot.reshape(1, -1), embedding_parent_index.reshape(1, -1))


def body(embeddings, embedding_parent_index, parent_slot, centroids):
    width = embeddings.shape[1]
    children, owned, _ = centroids.shape
    nodes = lax.axis_size("node")
    outers = lax.axis_size("outer")
    devices = nodes * outers
    shrink = 1.0 / (softness_level * width)
    node = lax.axis_index("node")
    everyone = ("node", "outer")
    rank = lax.axis_index(everyone)

    own = lax.dynamic_slice_in_dim(centroids, node * OWN, OWN, 1).transpose(1, 0, 2)
    unit = unit_scale(own.astype(jnp.float32))
    low = unit.astype(jnp.bfloat16)
    places, spill, common = plan(
        parent_slot, embedding_parent_index, rank.reshape(1), outers, nodes
    )
    packed = dense_pack(embeddings, (places, spill), common, outers, owned, devices)
    packed, unit, low, embeddings, places, me, here = lax.optimization_barrier(
        (packed, unit, low, embeddings, places, rank.reshape(1), node.reshape(1))
    )
    arrived = lax.all_to_all(
        packed.reshape(devices, SHORT, width), everyone, split_axis=0, concat_axis=0, tiled=True
    )
    late, notes, unfit = collect(arrived, me, nodes)
    unfit, unit, low, embeddings, places, here = lax.optimization_barrier(
        (unfit, unit, low, embeddings, places, here)
    )

    def short_way():
        arrivals = lax.all_to_all(late, "node", split_axis=0, concat_axis=0, tiled=True)
        flat = low.reshape(OWN * children, width)
        total = dense_sums(arrived.reshape(devices * SHORT, width), notes, flat, shrink)
        return finish(
            total, arrivals.reshape(nodes * SHORT, width), flat, unit, here, shrink, nodes
        )

    def long_way():
        full = pack(embeddings, places[0], places[1], outers, owned, devices)
        full = lax.all_to_all(
            full.reshape(devices, ROWS, width), everyone, split_axis=0, concat_axis=0, tiled=True
        )
        return child_sums(full.reshape(devices * ROWS, width), low, unit, shrink, nodes)

    fresh = lax.cond(unfit[0] > 0, long_way, short_way)
    received = lax.all_to_all(fresh, "node", split_axis=0, concat_axis=0, tiled=True)
    return put_in_order(received, children // nodes)


def solution(mesh):
    placed = (P(("node", "outer"), None), P(("node", "outer")), P(), P(None, "outer", None))
    return jax.shard_map(
        body,
        mesh=mesh,
        in_specs=placed,
        out_specs=(P("node", "outer", None), P("outer", None)),
        check_vma=False,
    )
```

```python
import functools

import jax
import jax.numpy as jnp
from jax import lax
from jax.experimental import pallas as pl
from jax.experimental.pallas import tpu as pltpu
from jax.sharding import PartitionSpec as P

softness_level = 0.1
prior_weight = 0.25
EPS = 1e-06

CAP = 12
OWN = 4
ROWS = OWN * CAP
TILE = 16
GROUPS = ROWS // TILE
PAIRS = 4
WIN = 32
SHORT = 32
GUESTS = 2
DENSE_PAIRS = 8
LANES = 128
NOBODY = 64


def unit_scale(values):
    return values * lax.rsqrt(jnp.mean(values * values, axis=-1, keepdims=True) + EPS)


def pack_kernel(outers, owned, start_ref, count_ref, rows_ref, out_ref, unit_ref):
    total, width = rows_ref.shape
    step = pl.program_id(0)
    chunk = 64

    @pl.when(step == 0)
    def _():
        unit_ref[total:, :] = jnp.zeros((unit_ref.shape[0] - total, width), jnp.bfloat16)

        def normalise(i, carry):
            at = pl.ds(pl.multiple_of(i * chunk, chunk), chunk)
            unit_ref[at, :] = unit_scale(rows_ref[at, :].astype(jnp.float32)).astype(jnp.bfloat16)
            return carry

        lax.fori_loop(0, total // chunk, normalise, 0, unroll=4)

    row = lax.broadcasted_iota(jnp.int32, (2 * ROWS, 1), 0)
    half = (row >= ROWS).astype(jnp.int32)
    inner = row - half * ROWS
    group = lax.shift_right_logical(inner, 4)
    place = inner & (TILE - 1)
    first = place < CAP
    source = half * OWN + jnp.where(first, group, OWN - 1)
    position = jnp.where(first, place, group * (TILE - CAP) + place - CAP)
    column = lax.broadcasted_iota(jnp.int32, (2 * ROWS, 2 * OWN * WIN), 1)
    for pair in range(PAIRS):
        target = jnp.full((2 * ROWS, 1), -1, jnp.int32)
        windows = []
        for q in range(2 * OWN):
            device = (step * PAIRS + pair) * 2 + q // OWN
            slot = lax.rem(device, outers) * owned + lax.div(device, outers) * OWN + q % OWN
            start = start_ref[slot]
            count = count_ref[slot]
            aligned = lax.shift_left(lax.shift_right_logical(start, 4), 4)
            windows.append(unit_ref[pl.ds(pl.multiple_of(aligned, TILE), WIN), :])
            spot = q * WIN + (start - aligned) + position
            target = jnp.where((source == q) & (position < count), spot, target)
        selector = (column == target).astype(jnp.float32).astype(jnp.bfloat16)
        window = jnp.concatenate(windows, axis=0)
        out_ref[pair * 2 * ROWS : (pair + 1) * 2 * ROWS, :] = jnp.dot(
            selector, window, preferred_element_type=jnp.float32
        ).astype(jnp.bfloat16)


def pack(embeddings, starts, counts, outers, owned, devices):
    total, width = embeddings.shape
    return pl.pallas_call(
        functools.partial(pack_kernel, outers, owned),
        out_shape=jax.ShapeDtypeStruct((devices * ROWS, width), jnp.bfloat16),
        grid_spec=pltpu.PrefetchScalarGridSpec(
            num_scalar_prefetch=2,
            grid=(devices // (2 * PAIRS),),
            in_specs=[
                pl.BlockSpec((total, width), lambda i, s, c: (0, 0), pipeline_mode=pl.Buffered(1))
            ],
            out_specs=pl.BlockSpec((2 * ROWS * PAIRS, width), lambda i, s, c: (i, 0)),
            scratch_shapes=[pltpu.VMEM((total + WIN, width), jnp.bfloat16)],
        ),
        compiler_params=pltpu.CompilerParams(vmem_limit_bytes=40 << 20),
        name="pack",
    )(starts, counts, embeddings)


def sums_kernel(shrink, per_node, rows_ref, low_ref, unit_ref, out_ref, total_ref):
    step = pl.program_id(0)
    block, width = rows_ref.shape
    sources = block // ROWS
    children = low_ref.shape[1]

    @pl.when(step == 0)
    def _():
        total_ref[...] = jnp.zeros_like(total_ref)

    lane = lax.broadcasted_iota(jnp.int32, (1, sources * TILE), 1)
    first = (lane & (TILE - 1)) < CAP
    for g in range(GROUPS):
        rows = jnp.concatenate(
            [rows_ref[b * ROWS + g * TILE : b * ROWS + (g + 1) * TILE, :] for b in range(sources)],
            axis=0,
        )
        low = jnp.concatenate([low_ref[g], low_ref[OWN - 1]], axis=0)
        logits = lax.dot_general(
            low, rows, (((1,), (1,)), ((), ())), preferred_element_type=jnp.float32
        )
        chosen = jnp.where(first, logits[:children], logits[children:]) * shrink
        raised = jnp.exp(chosen)
        weights = raised / jnp.sum(raised, axis=0, keepdims=True)
        zero = jnp.zeros_like(weights)
        paired = jnp.concatenate(
            [jnp.where(first, weights, zero), jnp.where(first, zero, weights)], axis=0
        ).astype(jnp.bfloat16)
        sums = jnp.dot(paired, rows, preferred_element_type=jnp.float32)
        total_ref[g] += sums[:children]
        total_ref[OWN - 1] += sums[children:]

    @pl.when(step == pl.num_programs(0) - 1)
    def _():
        parents = []
        for j in range(OWN):
            fresh = unit_scale(prior_weight * unit_ref[j] + total_ref[j])
            parents.append(unit_scale(jnp.sum(fresh, axis=0, keepdims=True)))
            fresh = fresh.astype(jnp.bfloat16)
            for m in range(children // per_node):
                out_ref[m, j * per_node : (j + 1) * per_node, :] = fresh[
                    m * per_node : (m + 1) * per_node
                ]
        tail = jnp.concatenate(parents + parents, axis=0).astype(jnp.bfloat16)
        for m in range(children // per_node):
            out_ref[m, OWN * per_node :, :] = tail


def child_sums(arrived, low, unit, shrink, nodes):
    total, width = arrived.shape
    children = low.shape[1]
    per_node = children // nodes
    block = 32 * ROWS
    whole = lambda i: (0, 0, 0)
    return pl.pallas_call(
        functools.partial(sums_kernel, shrink, per_node),
        out_shape=jax.ShapeDtypeStruct((nodes, OWN * per_node + 2 * OWN, width), jnp.bfloat16),
        grid=(total // block,),
        in_specs=[
            pl.BlockSpec((block, width), lambda i: (i, 0)),
            pl.BlockSpec(low.shape, whole, pipeline_mode=pl.Buffered(1)),
            pl.BlockSpec(unit.shape, whole, pipeline_mode=pl.Buffered(1)),
        ],
        out_specs=pl.BlockSpec((nodes, OWN * per_node + 2 * OWN, width), whole),
        scratch_shapes=[pltpu.VMEM((OWN, children, width), jnp.float32)],
        compiler_params=pltpu.CompilerParams(vmem_limit_bytes=48 << 20),
        name="child_sums",
    )(arrived, low, unit)


def order_kernel(per_node, rows_ref, children_ref, parents_ref):
    block = OWN * per_node + 2 * OWN
    nodes = rows_ref.shape[0] // block
    slots = nodes * OWN
    column = lax.broadcasted_iota(jnp.int32, (1, rows_ref.shape[0]), 1)
    out = lax.broadcasted_iota(jnp.int32, (per_node * slots, 1), 0)
    slot = out & (slots - 1)
    child = lax.div(out, slots)
    wanted = lax.div(slot, OWN) * block + (slot & (OWN - 1)) * per_node + child
    mover = (wanted == column).astype(jnp.float32).astype(jnp.bfloat16)
    rows = rows_ref[...]
    children_ref[...] = jnp.dot(mover, rows, preferred_element_type=jnp.float32)
    slot = lax.broadcasted_iota(jnp.int32, (slots, 1), 0)
    wanted = lax.div(slot, OWN) * block + OWN * per_node + (slot & (OWN - 1))
    mover = (wanted == column).astype(jnp.float32).astype(jnp.bfloat16)
    parents_ref[...] = jnp.dot(mover, rows, preferred_element_type=jnp.float32)


def put_in_order(received, per_node):
    nodes, block, width = received.shape
    slots = nodes * OWN
    children, parents = pl.pallas_call(
        functools.partial(order_kernel, per_node),
        out_shape=(
            jax.ShapeDtypeStruct((per_node * slots, width), jnp.float32),
            jax.ShapeDtypeStruct((slots, width), jnp.float32),
        ),
        name="put_in_order",
    )(received.reshape(nodes * block, width))
    return children.reshape(per_node, slots, width), parents


def dense_pack_kernel(
    outers,
    owned,
    start_ref,
    count_ref,
    guests_ref,
    turn_ref,
    hosts_ref,
    spill_ref,
    node_ref,
    rows_ref,
    common_ref,
    centroid_ref,
    out_ref,
    low_ref,
    unit_ref,
    wide_ref,
):
    total, width = rows_ref.shape
    step = pl.program_id(0)
    outer_bits = outers.bit_length() - 1
    centroids = centroid_ref[...].astype(jnp.float32).reshape(wide_ref.shape[1], width)
    for c in range(width // LANES):
        wide_ref[c] = centroids[:, c * LANES : (c + 1) * LANES]
    for j in range(OWN):
        at = OWN * (node_ref[0] & 1) + j
        few = wide_ref.shape[1] // 8
        mine = [wide_ref[c, pl.ds(at, few, stride=8), :] for c in range(width // LANES)]
        unit = unit_scale(jnp.concatenate(mine, axis=1))
        unit_ref[j] = unit
        low_ref[j] = unit.astype(jnp.bfloat16)

    place = lax.broadcasted_iota(jnp.int32, (SHORT, 1), 0) - 1
    column = lax.broadcasted_iota(jnp.int32, (SHORT, 2 * OWN * WIN), 1)
    lane = lax.broadcasted_iota(jnp.int32, (1, LANES), 1)
    lane_place = (lane & (SHORT - 1)) - 1
    top = lax.broadcasted_iota(jnp.int32, (8, 1), 0) == 0
    filler = jnp.zeros((1, width - 3 * LANES), jnp.float32)
    notes = jnp.concatenate([common_ref[0:1, :], common_ref[1:2, :], filler], axis=1)
    for pair in range(DENSE_PAIRS):
        windows = []
        selectors = []
        heads = []
        for h in range(2):
            device = (step * DENSE_PAIRS + pair) * 2 + h
            base = (device & (outers - 1)) * owned + (device >> outer_bits) * OWN
            at = jnp.int32(0)
            target = jnp.full((SHORT, 1), -1, jnp.int32)
            slots = jnp.full((1, LANES), NOBODY, jnp.int32)
            for j in range(OWN):
                start = start_ref[base + j]
                aligned = lax.shift_left(lax.shift_right_logical(start, 4), 4)
                aligned = jnp.minimum(aligned, total - WIN)
                windows.append(rows_ref[pl.ds(pl.multiple_of(aligned, TILE), WIN), :])
                spot = (h * OWN + j) * WIN + (start - aligned) - at
                target = jnp.where(place >= at, place + spot, target)
                slots = jnp.where(lane_place >= at, j, slots)
                at = at + count_ref[base + j]
            target = jnp.where(place < at, target, -1)
            slots = jnp.where(lane_place < at, slots, NOBODY)
            selectors.append(jnp.where(column == target, 1.0, 0.0).astype(jnp.bfloat16))
            heads.append(jnp.concatenate([slots.astype(jnp.float32), notes], axis=1))
        moved = unit_scale(
            jnp.dot(
                jnp.concatenate(selectors, axis=0),
                jnp.concatenate(windows, axis=0),
                preferred_element_type=jnp.float32,
            )
        )
        pieces = []
        for h in range(2):
            pieces.append(jnp.where(top, heads[h], moved[h * SHORT : h * SHORT + 8]))
            pieces.append(moved[h * SHORT + 8 : (h + 1) * SHORT])
        out_ref[pair * 2 * SHORT : (pair + 1) * 2 * SHORT, :] = jnp.concatenate(
            pieces, axis=0
        ).astype(jnp.bfloat16)

    tile_row = lax.broadcasted_iota(jnp.int32, (TILE, 1), 0)

    def base_of(m):
        device = step * 2 * DENSE_PAIRS + m
        return (device & (outers - 1)) * owned + (device >> outer_bits) * OWN

    def seat(m, carry):
        base = base_of(m)
        outer = lax.div(base, owned)
        for i in range(GUESTS):

            @pl.when(guests_ref[base] > i)
            def _():
                entry = turn_ref[base] + i * hosts_ref[base]
                source = spill_ref[outer, entry]
                slot = spill_ref[outers + outer, entry].astype(jnp.float32)
                aligned = lax.shift_left(lax.shift_right_logical(source, 4), 4)
                tile = rows_ref[pl.ds(pl.multiple_of(aligned, TILE), TILE), :].astype(jnp.float32)
                chosen = unit_scale(
                    jnp.sum(
                        jnp.where(tile_row == source - aligned, tile, 0.0), axis=0, keepdims=True
                    )
                )
                tail = pl.ds(pl.multiple_of(m * SHORT + TILE, TILE), TILE)
                kept = out_ref[tail, :].astype(jnp.float32)
                out_ref[tail, :] = jnp.where(tile_row == TILE - 1 - i, chosen, kept).astype(
                    jnp.bfloat16
                )
                head = pl.ds(pl.multiple_of(m * SHORT, TILE), TILE)
                where = slice(3 * LANES, 4 * LANES)
                kept = out_ref[head, where].astype(jnp.float32)
                mine = (tile_row == 0) & ((lane & 7) == 7 - i)
                out_ref[head, where] = jnp.where(mine, slot, kept).astype(jnp.bfloat16)

        return carry

    seated = guests_ref[base_of(0)]
    for m in range(1, 2 * DENSE_PAIRS):
        seated = seated + guests_ref[base_of(m)]

    @pl.when(seated > 0)
    def _():
        lax.fori_loop(0, 2 * DENSE_PAIRS, seat, 0)


def dense_pack(embeddings, scalars, common, centroids, outers, devices):
    total, width = embeddings.shape
    children, owned, _ = centroids.shape
    block = 2 * SHORT * DENSE_PAIRS
    steps = devices // (2 * DENSE_PAIRS)
    few = children // steps
    finished = pl.BlockSpec((OWN, few, width), lambda i, *_: (0, i, 0))
    return pl.pallas_call(
        functools.partial(dense_pack_kernel, outers, owned),
        out_shape=(
            pltpu.HBM((devices * SHORT, width), jnp.bfloat16),
            jax.ShapeDtypeStruct((OWN, children, width), jnp.bfloat16),
            jax.ShapeDtypeStruct((OWN, children, width), jnp.float32),
        ),
        grid_spec=pltpu.PrefetchScalarGridSpec(
            num_scalar_prefetch=len(scalars),
            grid=(steps,),
            in_specs=[
                pl.BlockSpec((total, width), lambda i, *_: (0, 0), pipeline_mode=pl.Buffered(1)),
                pl.BlockSpec((2, LANES), lambda i, *_: (0, 0), pipeline_mode=pl.Buffered(1)),
                pl.BlockSpec((few, 8, width), lambda i, *p: (i, p[-1][0] >> 1, 0)),
            ],
            out_specs=(pl.BlockSpec((block, width), lambda i, *_: (i, 0)), finished, finished),
            scratch_shapes=[pltpu.VMEM((width // LANES, few * 8, LANES), jnp.float32)],
        ),
        compiler_params=pltpu.CompilerParams(vmem_limit_bytes=62 << 20),
        name="dense_pack",
    )(*scalars, embeddings, common, centroids)


def collect_kernel(me_ref, rows_ref, head_ref, late_ref, notes_ref, unfit_ref, wide_ref):
    sources = rows_ref.shape[0]
    width = rows_ref.shape[2]
    columns = sources * 8
    heads = head_ref[...].astype(jnp.float32).reshape(sources * 8, head_ref.shape[2])
    notes = []
    for q in range(wide_ref.shape[0]):
        wide_ref[q] = heads[:, q * LANES : (q + 1) * LANES]
        notes.append(wide_ref[q, pl.ds(0, sources, stride=8), :])
    notes = jnp.concatenate(notes, axis=1)
    notes_ref[...] = notes[:, :LANES]
    everyone = notes[:, LANES : 2 * LANES]
    crowded = jnp.max(jnp.sum(everyone, axis=0, keepdims=True)) > SHORT - 1
    failed = jnp.max(notes[:, 2 * LANES : 3 * LANES]) > 0.0
    unfit_ref[0] = (crowded | failed).astype(jnp.int32)

    lane = lax.broadcasted_iota(jnp.int32, (1, LANES), 1)
    guests = jnp.sum(jnp.where(lane == me_ref[0], everyone, 0.0), axis=1, keepdims=True)
    column = lax.broadcasted_iota(jnp.int32, (1, columns), 1)
    owner = lax.shift_right_logical(column, 3)
    source = lax.broadcasted_iota(jnp.int32, (sources, 1), 0)
    before = jnp.sum(jnp.where(source < owner, guests, 0.0), axis=0, keepdims=True)
    here = jnp.sum(jnp.where(source == owner, guests, 0.0), axis=0, keepdims=True)
    slots = jnp.concatenate([notes[:, 3 * LANES :]] * (columns // LANES), axis=1)
    slots = jnp.sum(jnp.where(source == owner, slots, 0.0), axis=0, keepdims=True)
    order = 7 - (column & 7)
    place = jnp.where(order < here.astype(jnp.int32), before.astype(jnp.int32) + order + 1, -1)
    wanted = lax.broadcasted_iota(jnp.int32, (LANES, 1), 0) & (SHORT - 1)
    selector = (wanted == place).astype(jnp.float32).astype(jnp.bfloat16)
    slots = jnp.broadcast_to(slots, (8, columns)).astype(jnp.bfloat16)
    head = lax.dot_general(
        slots, selector, (((1,), (1,)), ((), ())), preferred_element_type=jnp.float32
    )[0:1]
    head = jnp.concatenate([head] * (width // LANES), axis=1)
    rows = rows_ref[...].astype(jnp.float32).reshape(columns, width).astype(jnp.bfloat16)
    moved = jnp.dot(selector[:SHORT], rows, preferred_element_type=jnp.float32)
    top = lax.broadcasted_iota(jnp.int32, (SHORT, 1), 0) == 0
    moved = jnp.where(top, head, moved).astype(jnp.bfloat16)
    for n in range(late_ref.shape[0]):
        late_ref[n] = moved


def collect(arrived, me, nodes):
    sources, short, width = arrived.shape
    return pl.pallas_call(
        collect_kernel,
        out_shape=(
            jax.ShapeDtypeStruct((nodes, SHORT, width), jnp.bfloat16),
            jax.ShapeDtypeStruct((sources, LANES), jnp.float32),
            jax.ShapeDtypeStruct((1,), jnp.int32),
        ),
        grid_spec=pltpu.PrefetchScalarGridSpec(
            num_scalar_prefetch=1,
            grid=(1,),
            in_specs=[
                pl.BlockSpec((sources, 8, width), lambda i, m: (0, short // 8 - 1, 0)),
                pl.BlockSpec((sources, 8, 4 * LANES), lambda i, m: (0, 0, 0)),
            ],
            out_specs=(
                pl.BlockSpec((nodes, SHORT, width), lambda i, m: (0, 0, 0)),
                pl.BlockSpec((sources, LANES), lambda i, m: (0, 0)),
                pl.BlockSpec(memory_space=pltpu.SMEM),
            ),
            scratch_shapes=[pltpu.VMEM((4, sources * 8, LANES), jnp.float32)],
        ),
        compiler_params=pltpu.CompilerParams(vmem_limit_bytes=58 << 20),
        name="collect",
    )(me, arrived, arrived)


def weighted_rows(low, rows, slots, shrink, piece):
    children = low.shape[0] // OWN
    spread = []
    for at in range(0, rows.shape[0], piece):
        here = slots[:, at : at + piece]
        logits = lax.dot_general(
            low,
            rows[at : at + piece],
            (((1,), (1,)), ((), ())),
            preferred_element_type=jnp.float32,
        )
        chosen = jnp.zeros((children, piece), jnp.float32)
        for j in range(OWN):
            chosen = jnp.where(here == j, logits[j * children : (j + 1) * children], chosen)
        raised = jnp.exp(chosen * shrink)
        weights = raised / jnp.sum(raised, axis=0, keepdims=True)
        spread.append(
            jnp.concatenate(
                [jnp.where(here == j, weights, 0.0) for j in range(OWN)], axis=0
            ).astype(jnp.bfloat16)
        )
    spread = jnp.concatenate(spread, axis=1)
    return jnp.dot(spread, rows, preferred_element_type=jnp.float32)


def along_lanes(notes):
    count = notes.shape[0]
    column = lax.broadcasted_iota(jnp.int32, (1, count * SHORT), 1)
    source = lax.broadcasted_iota(jnp.int32, (count, 1), 0)
    wide = jnp.concatenate([notes] * (count * SHORT // LANES), axis=1)
    mine = source == lax.shift_right_logical(column, 5)
    return jnp.sum(jnp.where(mine, wide, 0.0), axis=0, keepdims=True).astype(jnp.int32)


def dense_sums_kernel(shrink, rows_ref, notes_ref, low_ref, total_ref):
    sums = weighted_rows(low_ref[...], rows_ref[...], along_lanes(notes_ref[...]), shrink, 256)

    @pl.when(pl.program_id(0) == 0)
    def _():
        total_ref[...] = sums

    @pl.when(pl.program_id(0) > 0)
    def _():
        total_ref[...] += sums


def dense_sums(arrived, notes, low, shrink):
    total, width = arrived.shape
    block = 64 * SHORT
    return pl.pallas_call(
        functools.partial(dense_sums_kernel, shrink),
        out_shape=jax.ShapeDtypeStruct(low.shape, jnp.float32),
        grid=(total // block,),
        in_specs=[
            pl.BlockSpec((block, width), lambda i: (i, 0)),
            pl.BlockSpec((block // SHORT, LANES), lambda i: (i, 0)),
            pl.BlockSpec(low.shape, lambda i: (0, 0), pipeline_mode=pl.Buffered(1)),
        ],
        out_specs=pl.BlockSpec(low.shape, lambda i: (0, 0)),
        compiler_params=pltpu.CompilerParams(vmem_limit_bytes=48 << 20),
        cost_estimate=pl.CostEstimate(
            flops=4 * total * width * low.shape[0],
            bytes_accessed=2 * total * width + 6 * low.size,
            transcendentals=total * low.shape[0] // OWN,
        ),
        name="dense_sums",
    )(arrived, notes, low)


def finish_kernel(shrink, per_node, node_ref, total_ref, late_ref, low_ref, unit_ref, out_ref):
    children = unit_ref.shape[1]
    late = late_ref.shape[0] // SHORT
    notes = jnp.concatenate(
        [
            late_ref[b * SHORT : b * SHORT + TILE, :LANES].astype(jnp.float32)[0:1]
            for b in range(late)
        ],
        axis=0,
    )
    slots = along_lanes(notes) - 1 - OWN * node_ref[0]
    added = weighted_rows(low_ref[...], late_ref[...], slots, shrink, 256)
    parents = []
    for j in range(OWN):
        at = slice(j * children, (j + 1) * children)
        fresh = unit_scale(prior_weight * unit_ref[j] + (total_ref[at, :] + added[at]))
        parents.append(unit_scale(jnp.sum(fresh, axis=0, keepdims=True)))
        fresh = fresh.astype(jnp.bfloat16)
        for m in range(children // per_node):
            out_ref[m, j * per_node : (j + 1) * per_node, :] = fresh[
                m * per_node : (m + 1) * per_node
            ]
    tail = jnp.concatenate(parents + parents, axis=0).astype(jnp.bfloat16)
    for m in range(children // per_node):
        out_ref[m, OWN * per_node :, :] = tail


def finish(total, late, low, unit, node, shrink, nodes):
    per_node = unit.shape[1] // nodes
    out = (nodes, OWN * per_node + 2 * OWN, late.shape[1])
    return pl.pallas_call(
        functools.partial(finish_kernel, shrink, per_node),
        out_shape=jax.ShapeDtypeStruct(out, jnp.bfloat16),
        in_specs=[pl.BlockSpec(memory_space=pltpu.SMEM)]
        + [pl.BlockSpec(memory_space=pltpu.VMEM)] * 4,
        compiler_params=pltpu.CompilerParams(vmem_limit_bytes=48 << 20),
        name="finish",
    )(node, total, late, low, unit)


def plan_kernel(
    outers,
    nodes,
    rank_ref,
    slot_ref,
    ids_ref,
    start_ref,
    count_ref,
    guests_ref,
    turn_ref,
    hosts_ref,
    spill_ref,
    common_ref,
):
    slots = slot_ref.shape[1]
    owned = slots // outers
    blocks = ids_ref.shape[0]
    room = SHORT - 1
    wide = (slots, LANES)
    row = lax.broadcasted_iota(jnp.int32, wide, 0)
    lane = lax.broadcasted_iota(jnp.int32, wide, 1)
    rows = row.astype(jnp.float32)
    ones = jnp.ones((LANES, LANES), jnp.bfloat16)

    def flag(mask):
        return jnp.where(mask, 1.0, 0.0).astype(jnp.bfloat16)

    def times(left, right):
        return jnp.dot(left, right.astype(jnp.bfloat16), preferred_element_type=jnp.float32)

    ids = jnp.concatenate(
        [
            ids_ref[...].astype(jnp.float32),
            jnp.full((LANES - blocks, LANES), slots, jnp.float32),
        ],
        axis=0,
    )
    last = jnp.broadcast_to(jnp.transpose(ids)[LANES - 1 :, :], (8, LANES))
    previous = pltpu.roll(last, 1, 1)[0:1]
    last = last[0:1]
    full = last < rows
    reached = (lane == 0) | (previous < rows)
    block = flag(reached & (last >= rows))
    upper = jnp.floor(ids * 0.5)
    inside = times(block, jnp.concatenate([upper, ids - 2.0 * upper], axis=1))
    inside = 2.0 * inside[:, :LANES] + inside[:, LANES:]
    begins = LANES * times(flag(full), ones) + times(flag(inside < rows), ones)
    ends = pltpu.roll(begins, slots - 1, 0)
    ends = jnp.where(row == slots - 1, float(blocks * LANES), ends)

    other = lax.broadcasted_iota(jnp.int32, (slots, slots), 0)
    mover = flag(slot_ref[...] == other)
    upper = jnp.floor(begins * (1.0 / TILE))
    moved = times(mover, jnp.concatenate([upper, begins - TILE * upper], axis=1))
    starts = TILE * moved[:, :LANES] + moved[:, LANES:]
    counts = times(mover, ends - begins)

    def within(mask, *values):
        parts = range(0, slots, LANES)
        side = [value[at : at + LANES] for value in values for at in parts]
        sums = times(flag(mask), jnp.concatenate(side, axis=1))
        sums = [sums[:, at : at + LANES] for at in range(0, sums.shape[1], LANES)]
        each = len(parts)
        return [
            jnp.concatenate(sums[v * each : (v + 1) * each], axis=0) for v in range(len(values))
        ]

    one = lax.broadcasted_iota(jnp.int32, (LANES, LANES), 0)
    two = lax.broadcasted_iota(jnp.int32, (LANES, LANES), 1)
    group_one, group_two = lax.shift_right_logical(one, 2), lax.shift_right_logical(two, 2)
    same_group = group_one == group_two
    same_outer = lax.div(one, owned) == lax.div(two, owned)
    (first,) = within(same_group & (two < one), counts)
    (sent,) = within(same_group, counts)
    over = jnp.maximum(sent - room, 0.0)
    host = jnp.where(sent <= room - GUESTS, 1.0, 0.0)
    once = jnp.where((row & (OWN - 1)) == 0, 1.0, 0.0)
    parts = (over * once, host * once)
    over_first, host_first = within(same_outer & (group_two < group_one), *parts)
    overs, real_hosts = within(same_outer, *parts)
    hosts = jnp.maximum(real_hosts, 1.0)
    shift = jnp.zeros_like(hosts)
    for h in range(1, nodes + 1):
        shift = jnp.where(hosts == h, lax.rem(rank_ref[0], h).astype(jnp.float32), shift)
    turn = host_first - shift
    turn = jnp.where(turn < 0.0, turn + hosts, turn)
    guests = host * (
        jnp.where(overs > turn, 1.0, 0.0) + jnp.where(overs > turn + hosts, 1.0, 0.0)
    )
    failed = jnp.max(overs - GUESTS * real_hosts) > 0.0

    flat = jnp.zeros(wide, jnp.float32)
    for q, value in enumerate([starts, counts, guests, turn, hosts]):
        flat = jnp.where(lane == q, value, flat)
    flat = jnp.transpose(flat)[:8].astype(jnp.int32)
    for q, ref in enumerate([start_ref, count_ref, guests_ref, turn_ref, hosts_ref]):
        ref[...] = flat[q : q + 1].reshape(slots)

    begin = over_first + jnp.maximum(first - room, 0.0)
    end = over_first + jnp.maximum(first + counts - room, 0.0)
    entry = lane.astype(jnp.float32)
    held = (begin <= entry) & (entry < end)
    source = jnp.where(held, starts - first + room - over_first + entry, 0.0)
    named = jnp.where(held, ((row & (owned - 1)) + 1).astype(jnp.float32), 0.0)
    for o in range(outers):
        at = slice(o * owned, (o + 1) * owned)
        spill_ref[o : o + 1, :] = jnp.sum(source[at], axis=0, keepdims=True).astype(jnp.int32)
        spill_ref[outers + o : outers + o + 1, :] = jnp.sum(
            named[at], axis=0, keepdims=True
        ).astype(jnp.int32)
    device = (lane & (outers - 1)) * owned + lax.div(lane, outers) * OWN
    common_ref[0:1, :] = jnp.sum(jnp.where(row == device, guests, 0.0), axis=0, keepdims=True)
    common_ref[1:2, :] = jnp.broadcast_to(failed.astype(jnp.float32), (1, LANES))


def plan(parent_slot, embedding_parent_index, rank, outers, nodes):
    slots = parent_slot.shape[0]
    return pl.pallas_call(
        functools.partial(plan_kernel, outers, nodes),
        out_shape=(
            *[pltpu.HBM((slots,), jnp.int32)] * 5,
            pltpu.HBM((2 * outers, LANES), jnp.int32),
            jax.ShapeDtypeStruct((2, LANES), jnp.float32),
        ),
        in_specs=[pl.BlockSpec(memory_space=pltpu.SMEM)]
        + [pl.BlockSpec(memory_space=pltpu.VMEM)] * 2,
        name="plan",
    )(rank, parent_slot.reshape(1, -1), embedding_parent_index.reshape(-1, LANES))


def body(embeddings, embedding_parent_index, parent_slot, centroids):
    width = embeddings.shape[1]
    children, owned, _ = centroids.shape
    nodes = lax.axis_size("node")
    outers = lax.axis_size("outer")
    devices = nodes * outers
    shrink = 1.0 / (softness_level * width)
    node = lax.axis_index("node")
    everyone = ("node", "outer")
    rank = lax.axis_index(everyone)

    me, here = rank.reshape(1), node.reshape(1)
    *places, common = plan(parent_slot, embedding_parent_index, me, outers, nodes)
    packed, low, unit = dense_pack(
        embeddings, (*places, here), common, centroids, outers, devices
    )
    packed, unit, low, embeddings, starts, counts, me, here = lax.optimization_barrier(
        (packed, unit, low, embeddings, *places[:2], me, here)
    )
    arrived = lax.all_to_all(
        packed.reshape(devices, SHORT, width), everyone, split_axis=0, concat_axis=0, tiled=True
    )
    late, notes, unfit = collect(arrived, me, nodes)
    unfit, unit, low, embeddings, starts, counts, here = lax.optimization_barrier(
        (unfit, unit, low, embeddings, starts, counts, here)
    )

    def short_way():
        arrivals = lax.all_to_all(late, "node", split_axis=0, concat_axis=0, tiled=True)
        flat = low.reshape(OWN * children, width)
        total = dense_sums(arrived.reshape(devices * SHORT, width), notes, flat, shrink)
        return finish(
            total, arrivals.reshape(nodes * SHORT, width), flat, unit, here, shrink, nodes
        )

    def long_way():
        full = pack(embeddings, starts, counts, outers, owned, devices)
        full = lax.all_to_all(
            full.reshape(devices, ROWS, width), everyone, split_axis=0, concat_axis=0, tiled=True
        )
        return child_sums(full.reshape(devices * ROWS, width), low, unit, shrink, nodes)

    fresh = lax.cond(unfit[0] > 0, long_way, short_way)
    received = lax.all_to_all(fresh, "node", split_axis=0, concat_axis=0, tiled=True)
    return put_in_order(received, children // nodes)


def solution(mesh):
    placed = (P(("node", "outer"), None), P(("node", "outer")), P(), P(None, "outer", None))
    return jax.shard_map(
        body,
        mesh=mesh,
        in_specs=placed,
        out_specs=(P("node", "outer", None), P("outer", None)),
        check_vma=False,
    )
```

```python
import functools

import jax
import jax.numpy as jnp
from jax import lax
from jax.experimental import pallas as pl
from jax.experimental.pallas import tpu as pltpu
from jax.sharding import PartitionSpec as P

softness_level = 0.1
prior_weight = 0.25
EPS = 1e-06

CAP = 12
OWN = 4
ROWS = OWN * CAP
TILE = 16
GROUPS = ROWS // TILE
PAIRS = 4
WIN = 32
SHORT = 32
GUESTS = 2
DENSE_PAIRS = 8
LANES = 128
NOBODY = 64


def unit_scale(values):
    return values * lax.rsqrt(jnp.mean(values * values, axis=-1, keepdims=True) + EPS)


def pack_kernel(outers, owned, start_ref, count_ref, rows_ref, out_ref, unit_ref):
    total, width = rows_ref.shape
    step = pl.program_id(0)
    chunk = 64

    @pl.when(step == 0)
    def _():
        unit_ref[total:, :] = jnp.zeros((unit_ref.shape[0] - total, width), jnp.bfloat16)

        def normalise(i, carry):
            at = pl.ds(pl.multiple_of(i * chunk, chunk), chunk)
            unit_ref[at, :] = unit_scale(rows_ref[at, :].astype(jnp.float32)).astype(jnp.bfloat16)
            return carry

        lax.fori_loop(0, total // chunk, normalise, 0, unroll=4)

    row = lax.broadcasted_iota(jnp.int32, (2 * ROWS, 1), 0)
    half = (row >= ROWS).astype(jnp.int32)
    inner = row - half * ROWS
    group = lax.shift_right_logical(inner, 4)
    place = inner & (TILE - 1)
    first = place < CAP
    source = half * OWN + jnp.where(first, group, OWN - 1)
    position = jnp.where(first, place, group * (TILE - CAP) + place - CAP)
    column = lax.broadcasted_iota(jnp.int32, (2 * ROWS, 2 * OWN * WIN), 1)
    for pair in range(PAIRS):
        target = jnp.full((2 * ROWS, 1), -1, jnp.int32)
        windows = []
        for q in range(2 * OWN):
            device = (step * PAIRS + pair) * 2 + q // OWN
            slot = lax.rem(device, outers) * owned + lax.div(device, outers) * OWN + q % OWN
            start = start_ref[slot]
            count = count_ref[slot]
            aligned = lax.shift_left(lax.shift_right_logical(start, 4), 4)
            windows.append(unit_ref[pl.ds(pl.multiple_of(aligned, TILE), WIN), :])
            spot = q * WIN + (start - aligned) + position
            target = jnp.where((source == q) & (position < count), spot, target)
        selector = (column == target).astype(jnp.float32).astype(jnp.bfloat16)
        window = jnp.concatenate(windows, axis=0)
        out_ref[pair * 2 * ROWS : (pair + 1) * 2 * ROWS, :] = jnp.dot(
            selector, window, preferred_element_type=jnp.float32
        ).astype(jnp.bfloat16)


def pack(embeddings, starts, counts, outers, owned, devices):
    total, width = embeddings.shape
    return pl.pallas_call(
        functools.partial(pack_kernel, outers, owned),
        out_shape=jax.ShapeDtypeStruct((devices * ROWS, width), jnp.bfloat16),
        grid_spec=pltpu.PrefetchScalarGridSpec(
            num_scalar_prefetch=2,
            grid=(devices // (2 * PAIRS),),
            in_specs=[
                pl.BlockSpec((total, width), lambda i, s, c: (0, 0), pipeline_mode=pl.Buffered(1))
            ],
            out_specs=pl.BlockSpec((2 * ROWS * PAIRS, width), lambda i, s, c: (i, 0)),
            scratch_shapes=[pltpu.VMEM((total + WIN, width), jnp.bfloat16)],
        ),
        compiler_params=pltpu.CompilerParams(vmem_limit_bytes=40 << 20),
        name="pack",
    )(starts, counts, embeddings)


def sums_kernel(shrink, per_node, rows_ref, low_ref, unit_ref, out_ref, total_ref):
    step = pl.program_id(0)
    block, width = rows_ref.shape
    sources = block // ROWS
    children = low_ref.shape[1]

    @pl.when(step == 0)
    def _():
        total_ref[...] = jnp.zeros_like(total_ref)

    lane = lax.broadcasted_iota(jnp.int32, (1, sources * TILE), 1)
    first = (lane & (TILE - 1)) < CAP
    for g in range(GROUPS):
        rows = jnp.concatenate(
            [rows_ref[b * ROWS + g * TILE : b * ROWS + (g + 1) * TILE, :] for b in range(sources)],
            axis=0,
        )
        low = jnp.concatenate([low_ref[g], low_ref[OWN - 1]], axis=0)
        logits = lax.dot_general(
            low, rows, (((1,), (1,)), ((), ())), preferred_element_type=jnp.float32
        )
        chosen = jnp.where(first, logits[:children], logits[children:]) * shrink
        raised = jnp.exp(chosen)
        weights = raised / jnp.sum(raised, axis=0, keepdims=True)
        zero = jnp.zeros_like(weights)
        paired = jnp.concatenate(
            [jnp.where(first, weights, zero), jnp.where(first, zero, weights)], axis=0
        ).astype(jnp.bfloat16)
        sums = jnp.dot(paired, rows, preferred_element_type=jnp.float32)
        total_ref[g] += sums[:children]
        total_ref[OWN - 1] += sums[children:]

    @pl.when(step == pl.num_programs(0) - 1)
    def _():
        parents = []
        for j in range(OWN):
            fresh = unit_scale(prior_weight * unit_ref[j] + total_ref[j])
            parents.append(unit_scale(jnp.sum(fresh, axis=0, keepdims=True)))
            fresh = fresh.astype(jnp.bfloat16)
            for m in range(children // per_node):
                out_ref[m, j * per_node : (j + 1) * per_node, :] = fresh[
                    m * per_node : (m + 1) * per_node
                ]
        tail = jnp.concatenate(parents + parents, axis=0).astype(jnp.bfloat16)
        for m in range(children // per_node):
            out_ref[m, OWN * per_node :, :] = tail


def child_sums(arrived, low, unit, shrink, nodes):
    total, width = arrived.shape
    children = low.shape[1]
    per_node = children // nodes
    block = 32 * ROWS
    whole = lambda i: (0, 0, 0)
    return pl.pallas_call(
        functools.partial(sums_kernel, shrink, per_node),
        out_shape=jax.ShapeDtypeStruct((nodes, OWN * per_node + 2 * OWN, width), jnp.bfloat16),
        grid=(total // block,),
        in_specs=[
            pl.BlockSpec((block, width), lambda i: (i, 0)),
            pl.BlockSpec(low.shape, whole, pipeline_mode=pl.Buffered(1)),
            pl.BlockSpec(unit.shape, whole, pipeline_mode=pl.Buffered(1)),
        ],
        out_specs=pl.BlockSpec((nodes, OWN * per_node + 2 * OWN, width), whole),
        scratch_shapes=[pltpu.VMEM((OWN, children, width), jnp.float32)],
        compiler_params=pltpu.CompilerParams(vmem_limit_bytes=48 << 20),
        name="child_sums",
    )(arrived, low, unit)


def order_kernel(per_node, rows_ref, children_ref, parents_ref):
    block = OWN * per_node + 2 * OWN
    nodes = rows_ref.shape[0] // block
    slots = nodes * OWN
    column = lax.broadcasted_iota(jnp.int32, (1, rows_ref.shape[0]), 1)
    out = lax.broadcasted_iota(jnp.int32, (per_node * slots, 1), 0)
    slot = out & (slots - 1)
    child = lax.div(out, slots)
    wanted = lax.div(slot, OWN) * block + (slot & (OWN - 1)) * per_node + child
    mover = (wanted == column).astype(jnp.float32).astype(jnp.bfloat16)
    rows = rows_ref[...]
    children_ref[...] = jnp.dot(mover, rows, preferred_element_type=jnp.float32)
    slot = lax.broadcasted_iota(jnp.int32, (slots, 1), 0)
    wanted = lax.div(slot, OWN) * block + OWN * per_node + (slot & (OWN - 1))
    mover = (wanted == column).astype(jnp.float32).astype(jnp.bfloat16)
    parents_ref[...] = jnp.dot(mover, rows, preferred_element_type=jnp.float32)


def put_in_order(received, per_node):
    nodes, block, width = received.shape
    slots = nodes * OWN
    children, parents = pl.pallas_call(
        functools.partial(order_kernel, per_node),
        out_shape=(
            jax.ShapeDtypeStruct((per_node * slots, width), jnp.float32),
            jax.ShapeDtypeStruct((slots, width), jnp.float32),
        ),
        name="put_in_order",
    )(received.reshape(nodes * block, width))
    return children.reshape(per_node, slots, width), parents


def dense_pack_kernel(
    outers,
    owned,
    nodes,
    me_ref,
    node_ref,
    slot_ref,
    ids_ref,
    far_rows_ref,
    centroid_ref,
    out_ref,
    low_ref,
    unit_ref,
    rows_ref,
    wide_ref,
    common_ref,
    *work,
):
    planned, placed, done = work[:6], work[6:12], work[12]
    start_ref, count_ref, guests_ref, turn_ref, hosts_ref, spill_ref = placed
    total, width = rows_ref.shape
    step = pl.program_id(0)

    @pl.when(step == 0)
    def _():
        fetch = pltpu.make_async_copy(far_rows_ref, rows_ref, done.at[len(placed)])
        fetch.start()
        plan_kernel(outers, nodes, me_ref, slot_ref, ids_ref, *planned, common_ref)

    outer_bits = outers.bit_length() - 1
    centroids = centroid_ref[...].astype(jnp.float32).reshape(wide_ref.shape[1], width)
    for c in range(width // LANES):
        wide_ref[c] = centroids[:, c * LANES : (c + 1) * LANES]
    for j in range(OWN):
        at = OWN * (node_ref[0] & 1) + j
        few = wide_ref.shape[1] // 8
        mine = [wide_ref[c, pl.ds(at, few, stride=8), :] for c in range(width // LANES)]
        unit = unit_scale(jnp.concatenate(mine, axis=1))
        unit_ref[j] = unit
        low_ref[j] = unit.astype(jnp.bfloat16)

    @pl.when(step == 0)
    def _():
        copies = [
            pltpu.make_async_copy(planned[i], placed[i], done.at[i]) for i in range(len(placed))
        ]
        for copy in copies:
            copy.start()
        for copy in copies:
            copy.wait()
        pltpu.make_async_copy(far_rows_ref, rows_ref, done.at[len(placed)]).wait()

    place = lax.broadcasted_iota(jnp.int32, (SHORT, 1), 0) - 1
    column = lax.broadcasted_iota(jnp.int32, (SHORT, 2 * OWN * WIN), 1)
    lane = lax.broadcasted_iota(jnp.int32, (1, LANES), 1)
    lane_place = (lane & (SHORT - 1)) - 1
    top = lax.broadcasted_iota(jnp.int32, (8, 1), 0) == 0
    filler = jnp.zeros((1, width - 3 * LANES), jnp.float32)
    notes = jnp.concatenate([common_ref[0:1, :], common_ref[1:2, :], filler], axis=1)
    for pair in range(DENSE_PAIRS):
        windows = []
        selectors = []
        heads = []
        for h in range(2):
            device = (step * DENSE_PAIRS + pair) * 2 + h
            base = (device & (outers - 1)) * owned + (device >> outer_bits) * OWN
            at = jnp.int32(0)
            target = jnp.full((SHORT, 1), -1, jnp.int32)
            slots = jnp.full((1, LANES), NOBODY, jnp.int32)
            for j in range(OWN):
                start = start_ref[base + j]
                aligned = lax.shift_left(lax.shift_right_logical(start, 4), 4)
                aligned = jnp.minimum(aligned, total - WIN)
                windows.append(rows_ref[pl.ds(pl.multiple_of(aligned, TILE), WIN), :])
                spot = (h * OWN + j) * WIN + (start - aligned) - at
                target = jnp.where(place >= at, place + spot, target)
                slots = jnp.where(lane_place >= at, j, slots)
                at = at + count_ref[base + j]
            target = jnp.where(place < at, target, -1)
            slots = jnp.where(lane_place < at, slots, NOBODY)
            selectors.append(jnp.where(column == target, 1.0, 0.0).astype(jnp.bfloat16))
            heads.append(jnp.concatenate([slots.astype(jnp.float32), notes], axis=1))
        moved = unit_scale(
            jnp.dot(
                jnp.concatenate(selectors, axis=0),
                jnp.concatenate(windows, axis=0),
                preferred_element_type=jnp.float32,
            )
        )
        pieces = []
        for h in range(2):
            pieces.append(jnp.where(top, heads[h], moved[h * SHORT : h * SHORT + 8]))
            pieces.append(moved[h * SHORT + 8 : (h + 1) * SHORT])
        out_ref[pair * 2 * SHORT : (pair + 1) * 2 * SHORT, :] = jnp.concatenate(
            pieces, axis=0
        ).astype(jnp.bfloat16)

    tile_row = lax.broadcasted_iota(jnp.int32, (TILE, 1), 0)

    def base_of(m):
        device = step * 2 * DENSE_PAIRS + m
        return (device & (outers - 1)) * owned + (device >> outer_bits) * OWN

    def seat(m, base, i):
        outer = lax.shift_right_logical(base, owned.bit_length() - 1)
        entry = turn_ref[base] + i * hosts_ref[base]
        source = spill_ref[outer, entry]
        slot = spill_ref[outers + outer, entry].astype(jnp.float32)
        aligned = lax.shift_left(lax.shift_right_logical(source, 4), 4)
        tile = rows_ref[pl.ds(pl.multiple_of(aligned, TILE), TILE), :].astype(jnp.float32)
        chosen = unit_scale(
            jnp.sum(jnp.where(tile_row == source - aligned, tile, 0.0), axis=0, keepdims=True)
        )
        tail = slice(m * SHORT + TILE, (m + 1) * SHORT)
        kept = out_ref[tail, :].astype(jnp.float32)
        out_ref[tail, :] = jnp.where(tile_row == TILE - 1 - i, chosen, kept).astype(jnp.bfloat16)
        head = slice(m * SHORT, m * SHORT + TILE)
        where = slice(3 * LANES, 4 * LANES)
        kept = out_ref[head, where].astype(jnp.float32)
        mine = (tile_row == 0) & ((lane & 7) == 7 - i)
        out_ref[head, where] = jnp.where(mine, slot, kept).astype(jnp.bfloat16)

    bases = [base_of(m) for m in range(2 * DENSE_PAIRS)]
    seated = guests_ref[bases[0]]
    for base in bases[1:]:
        seated = seated + guests_ref[base]

    @pl.when(seated > 0)
    def _():
        for m, base in enumerate(bases):
            guests = guests_ref[base]

            @pl.when(guests > 0)
            def _():
                seat(m, base, 0)

                @pl.when(guests > 1)
                def _():
                    seat(m, base, 1)


def dense_pack(embeddings, parent_slot, ids, centroids, me, node, outers, nodes):
    total, width = embeddings.shape
    children, owned, _ = centroids.shape
    slots = parent_slot.shape[0]
    devices = outers * nodes
    block = 2 * SHORT * DENSE_PAIRS
    steps = devices // (2 * DENSE_PAIRS)
    few = children // steps
    finished = pl.BlockSpec((OWN, few, width), lambda i, *_: (0, i, 0))
    shapes = [(slots,)] * 5 + [(2 * outers, LANES)]
    return pl.pallas_call(
        functools.partial(dense_pack_kernel, outers, owned, nodes),
        out_shape=(
            pltpu.HBM((devices * SHORT, width), jnp.bfloat16),
            jax.ShapeDtypeStruct((OWN, children, width), jnp.bfloat16),
            jax.ShapeDtypeStruct((OWN, children, width), jnp.float32),
        ),
        grid_spec=pltpu.PrefetchScalarGridSpec(
            num_scalar_prefetch=2,
            grid=(steps,),
            in_specs=[
                pl.BlockSpec((1, slots), lambda i, *_: (0, 0), pipeline_mode=pl.Buffered(1)),
                pl.BlockSpec(
                    (total // LANES, LANES), lambda i, *_: (0, 0), pipeline_mode=pl.Buffered(1)
                ),
                pl.BlockSpec(memory_space=pltpu.HBM),
                pl.BlockSpec((few, 8, width), lambda i, m, n: (i, n[0] >> 1, 0)),
            ],
            out_specs=(pl.BlockSpec((block, width), lambda i, *_: (i, 0)), finished, finished),
            scratch_shapes=[
                pltpu.VMEM((total, width), jnp.bfloat16),
                pltpu.VMEM((width // LANES, few * 8, LANES), jnp.float32),
                pltpu.VMEM((2, LANES), jnp.float32),
                *[pltpu.VMEM(shape, jnp.int32) for shape in shapes],
                *[pltpu.SMEM(shape, jnp.int32) for shape in shapes],
                pltpu.SemaphoreType.DMA((len(shapes) + 1,)),
            ],
        ),
        compiler_params=pltpu.CompilerParams(vmem_limit_bytes=62 << 20),
        name="dense_pack",
    )(me, node, parent_slot.reshape(1, -1), ids.reshape(-1, LANES), embeddings, centroids)


def collect_kernel(me_ref, rows_ref, head_ref, late_ref, notes_ref, unfit_ref, wide_ref):
    sources = rows_ref.shape[0]
    width = rows_ref.shape[2]
    columns = sources * 8
    heads = head_ref[...].astype(jnp.float32).reshape(sources * 8, head_ref.shape[2])
    notes = []
    for q in range(wide_ref.shape[0]):
        wide_ref[q] = heads[:, q * LANES : (q + 1) * LANES]
        notes.append(wide_ref[q, pl.ds(0, sources, stride=8), :])
    notes = jnp.concatenate(notes, axis=1)
    notes_ref[...] = notes[:, :LANES]
    everyone = notes[:, LANES : 2 * LANES]
    crowded = jnp.max(jnp.sum(everyone, axis=0, keepdims=True)) > SHORT - 1
    failed = jnp.max(notes[:, 2 * LANES : 3 * LANES]) > 0.0
    unfit_ref[0] = (crowded | failed).astype(jnp.int32)

    lane = lax.broadcasted_iota(jnp.int32, (1, LANES), 1)
    guests = jnp.sum(jnp.where(lane == me_ref[0], everyone, 0.0), axis=1, keepdims=True)
    column = lax.broadcasted_iota(jnp.int32, (1, columns), 1)
    owner = lax.shift_right_logical(column, 3)
    source = lax.broadcasted_iota(jnp.int32, (sources, 1), 0)
    before = jnp.sum(jnp.where(source < owner, guests, 0.0), axis=0, keepdims=True)
    here = jnp.sum(jnp.where(source == owner, guests, 0.0), axis=0, keepdims=True)
    slots = jnp.concatenate([notes[:, 3 * LANES :]] * (columns // LANES), axis=1)
    slots = jnp.sum(jnp.where(source == owner, slots, 0.0), axis=0, keepdims=True)
    order = 7 - (column & 7)
    place = jnp.where(order < here.astype(jnp.int32), before.astype(jnp.int32) + order + 1, -1)
    wanted = lax.broadcasted_iota(jnp.int32, (LANES, 1), 0) & (SHORT - 1)
    selector = (wanted == place).astype(jnp.float32).astype(jnp.bfloat16)
    slots = jnp.broadcast_to(slots, (8, columns)).astype(jnp.bfloat16)
    head = lax.dot_general(
        slots, selector, (((1,), (1,)), ((), ())), preferred_element_type=jnp.float32
    )[0:1]
    head = jnp.concatenate([head] * (width // LANES), axis=1)
    rows = rows_ref[...].astype(jnp.float32).reshape(columns, width).astype(jnp.bfloat16)
    moved = jnp.dot(selector[:SHORT], rows, preferred_element_type=jnp.float32)
    top = lax.broadcasted_iota(jnp.int32, (SHORT, 1), 0) == 0
    moved = jnp.where(top, head, moved).astype(jnp.bfloat16)
    for n in range(late_ref.shape[0]):
        late_ref[n] = moved


def collect(arrived, me, nodes):
    sources, short, width = arrived.shape
    return pl.pallas_call(
        collect_kernel,
        out_shape=(
            jax.ShapeDtypeStruct((nodes, SHORT, width), jnp.bfloat16),
            jax.ShapeDtypeStruct((sources, LANES), jnp.float32),
            jax.ShapeDtypeStruct((1,), jnp.int32),
        ),
        grid_spec=pltpu.PrefetchScalarGridSpec(
            num_scalar_prefetch=1,
            grid=(1,),
            in_specs=[
                pl.BlockSpec((sources, 8, width), lambda i, m: (0, short // 8 - 1, 0)),
                pl.BlockSpec((sources, 8, 4 * LANES), lambda i, m: (0, 0, 0)),
            ],
            out_specs=(
                pl.BlockSpec((nodes, SHORT, width), lambda i, m: (0, 0, 0)),
                pl.BlockSpec((sources, LANES), lambda i, m: (0, 0)),
                pl.BlockSpec(memory_space=pltpu.SMEM),
            ),
            scratch_shapes=[pltpu.VMEM((4, sources * 8, LANES), jnp.float32)],
        ),
        compiler_params=pltpu.CompilerParams(vmem_limit_bytes=58 << 20),
        name="collect",
    )(me, arrived, arrived)


def weighted_rows(low, rows, slots, shrink, piece):
    children = low.shape[0] // OWN
    spread = []
    for at in range(0, rows.shape[0], piece):
        here = slots[:, at : at + piece]
        logits = lax.dot_general(
            low,
            rows[at : at + piece],
            (((1,), (1,)), ((), ())),
            preferred_element_type=jnp.float32,
        )
        chosen = jnp.zeros((children, piece), jnp.float32)
        for j in range(OWN):
            chosen = jnp.where(here == j, logits[j * children : (j + 1) * children], chosen)
        raised = jnp.exp(chosen * shrink)
        weights = raised / jnp.sum(raised, axis=0, keepdims=True)
        spread.append(
            jnp.concatenate(
                [jnp.where(here == j, weights, 0.0) for j in range(OWN)], axis=0
            ).astype(jnp.bfloat16)
        )
    spread = jnp.concatenate(spread, axis=1)
    return jnp.dot(spread, rows, preferred_element_type=jnp.float32)


def along_lanes(notes):
    count = notes.shape[0]
    column = lax.broadcasted_iota(jnp.int32, (1, count * SHORT), 1)
    source = lax.broadcasted_iota(jnp.int32, (count, 1), 0)
    wide = jnp.concatenate([notes] * (count * SHORT // LANES), axis=1)
    mine = source == lax.shift_right_logical(column, 5)
    return jnp.sum(jnp.where(mine, wide, 0.0), axis=0, keepdims=True).astype(jnp.int32)


def dense_sums_kernel(shrink, rows_ref, notes_ref, low_ref, total_ref):
    sums = weighted_rows(low_ref[...], rows_ref[...], along_lanes(notes_ref[...]), shrink, 256)

    @pl.when(pl.program_id(0) == 0)
    def _():
        total_ref[...] = sums

    @pl.when(pl.program_id(0) > 0)
    def _():
        total_ref[...] += sums


def dense_sums(arrived, notes, low, shrink):
    total, width = arrived.shape
    block = 64 * SHORT
    return pl.pallas_call(
        functools.partial(dense_sums_kernel, shrink),
        out_shape=jax.ShapeDtypeStruct(low.shape, jnp.float32),
        grid=(total // block,),
        in_specs=[
            pl.BlockSpec((block, width), lambda i: (i, 0)),
            pl.BlockSpec((block // SHORT, LANES), lambda i: (i, 0)),
            pl.BlockSpec(low.shape, lambda i: (0, 0), pipeline_mode=pl.Buffered(1)),
        ],
        out_specs=pl.BlockSpec(low.shape, lambda i: (0, 0)),
        compiler_params=pltpu.CompilerParams(vmem_limit_bytes=48 << 20),
        cost_estimate=pl.CostEstimate(
            flops=4 * total * width * low.shape[0],
            bytes_accessed=2 * total * width + 6 * low.size,
            transcendentals=total * low.shape[0] // OWN,
        ),
        name="dense_sums",
    )(arrived, notes, low)


def finish_kernel(shrink, per_node, node_ref, total_ref, late_ref, low_ref, unit_ref, out_ref):
    children = unit_ref.shape[1]
    late = late_ref.shape[0] // SHORT
    notes = jnp.concatenate(
        [
            late_ref[b * SHORT : b * SHORT + TILE, :LANES].astype(jnp.float32)[0:1]
            for b in range(late)
        ],
        axis=0,
    )
    slots = along_lanes(notes) - 1 - OWN * node_ref[0]
    added = weighted_rows(low_ref[...], late_ref[...], slots, shrink, 256)
    parents = []
    for j in range(OWN):
        at = slice(j * children, (j + 1) * children)
        fresh = unit_scale(prior_weight * unit_ref[j] + (total_ref[at, :] + added[at]))
        parents.append(unit_scale(jnp.sum(fresh, axis=0, keepdims=True)))
        fresh = fresh.astype(jnp.bfloat16)
        for m in range(children // per_node):
            out_ref[m, j * per_node : (j + 1) * per_node, :] = fresh[
                m * per_node : (m + 1) * per_node
            ]
    tail = jnp.concatenate(parents + parents, axis=0).astype(jnp.bfloat16)
    for m in range(children // per_node):
        out_ref[m, OWN * per_node :, :] = tail


def finish(total, late, low, unit, node, shrink, nodes):
    per_node = unit.shape[1] // nodes
    out = (nodes, OWN * per_node + 2 * OWN, late.shape[1])
    return pl.pallas_call(
        functools.partial(finish_kernel, shrink, per_node),
        out_shape=jax.ShapeDtypeStruct(out, jnp.bfloat16),
        in_specs=[pl.BlockSpec(memory_space=pltpu.SMEM)]
        + [pl.BlockSpec(memory_space=pltpu.VMEM)] * 4,
        compiler_params=pltpu.CompilerParams(vmem_limit_bytes=48 << 20),
        name="finish",
    )(node, total, late, low, unit)


def plan_kernel(
    outers,
    nodes,
    rank_ref,
    slot_ref,
    ids_ref,
    start_ref,
    count_ref,
    guests_ref,
    turn_ref,
    hosts_ref,
    spill_ref,
    common_ref,
):
    slots = slot_ref.shape[1]
    owned = slots // outers
    blocks = ids_ref.shape[0]
    room = SHORT - 1
    wide = (slots, LANES)
    row = lax.broadcasted_iota(jnp.int32, wide, 0)
    lane = lax.broadcasted_iota(jnp.int32, wide, 1)
    rows = row.astype(jnp.float32)
    ones = jnp.ones((LANES, LANES), jnp.bfloat16)

    def flag(mask):
        return jnp.where(mask, 1.0, 0.0).astype(jnp.bfloat16)

    def times(left, right):
        return jnp.dot(left, right.astype(jnp.bfloat16), preferred_element_type=jnp.float32)

    ids = jnp.concatenate(
        [
            ids_ref[...].astype(jnp.float32),
            jnp.full((LANES - blocks, LANES), slots, jnp.float32),
        ],
        axis=0,
    )
    last = jnp.broadcast_to(jnp.transpose(ids)[LANES - 1 :, :], (8, LANES))
    previous = pltpu.roll(last, 1, 1)[0:1]
    last = last[0:1]
    full = last < rows
    reached = (lane == 0) | (previous < rows)
    block = flag(reached & (last >= rows))
    upper = jnp.floor(ids * 0.5)
    inside = times(block, jnp.concatenate([upper, ids - 2.0 * upper], axis=1))
    inside = 2.0 * inside[:, :LANES] + inside[:, LANES:]
    begins = LANES * times(flag(full), ones) + times(flag(inside < rows), ones)
    ends = pltpu.roll(begins, slots - 1, 0)
    ends = jnp.where(row == slots - 1, float(blocks * LANES), ends)

    other = lax.broadcasted_iota(jnp.int32, (slots, slots), 0)
    mover = flag(slot_ref[...] == other)
    upper = jnp.floor(begins * (1.0 / TILE))
    moved = times(mover, jnp.concatenate([upper, begins - TILE * upper], axis=1))
    starts = TILE * moved[:, :LANES] + moved[:, LANES:]
    counts = times(mover, ends - begins)

    def within(mask, *values):
        parts = range(0, slots, LANES)
        side = [value[at : at + LANES] for value in values for at in parts]
        sums = times(flag(mask), jnp.concatenate(side, axis=1))
        sums = [sums[:, at : at + LANES] for at in range(0, sums.shape[1], LANES)]
        each = len(parts)
        return [
            jnp.concatenate(sums[v * each : (v + 1) * each], axis=0) for v in range(len(values))
        ]

    one = lax.broadcasted_iota(jnp.int32, (LANES, LANES), 0)
    two = lax.broadcasted_iota(jnp.int32, (LANES, LANES), 1)
    group_one, group_two = lax.shift_right_logical(one, 2), lax.shift_right_logical(two, 2)
    same_group = group_one == group_two
    same_outer = lax.div(one, owned) == lax.div(two, owned)
    (first,) = within(same_group & (two < one), counts)
    (sent,) = within(same_group, counts)
    over = jnp.maximum(sent - room, 0.0)
    host = jnp.where(sent <= room - GUESTS, 1.0, 0.0)
    once = jnp.where((row & (OWN - 1)) == 0, 1.0, 0.0)
    parts = (over * once, host * once)
    over_first, host_first = within(same_outer & (group_two < group_one), *parts)
    overs, real_hosts = within(same_outer, *parts)
    hosts = jnp.maximum(real_hosts, 1.0)
    shift = jnp.zeros_like(hosts)
    for h in range(1, nodes + 1):
        shift = jnp.where(hosts == h, lax.rem(rank_ref[0], h).astype(jnp.float32), shift)
    turn = host_first - shift
    turn = jnp.where(turn < 0.0, turn + hosts, turn)
    guests = host * (
        jnp.where(overs > turn, 1.0, 0.0) + jnp.where(overs > turn + hosts, 1.0, 0.0)
    )
    failed = jnp.max(overs - GUESTS * real_hosts) > 0.0

    flat = jnp.zeros(wide, jnp.float32)
    for q, value in enumerate([starts, counts, guests, turn, hosts]):
        flat = jnp.where(lane == q, value, flat)
    flat = jnp.transpose(flat)[:8].astype(jnp.int32)
    for q, ref in enumerate([start_ref, count_ref, guests_ref, turn_ref, hosts_ref]):
        ref[...] = flat[q : q + 1].reshape(slots)

    begin = over_first + jnp.maximum(first - room, 0.0)
    end = over_first + jnp.maximum(first + counts - room, 0.0)
    entry = lane.astype(jnp.float32)
    held = (begin <= entry) & (entry < end)
    source = jnp.where(held, starts - first + room - over_first + entry, 0.0)
    named = jnp.where(held, ((row & (owned - 1)) + 1).astype(jnp.float32), 0.0)
    for o in range(outers):
        at = slice(o * owned, (o + 1) * owned)
        spill_ref[o : o + 1, :] = jnp.sum(source[at], axis=0, keepdims=True).astype(jnp.int32)
        spill_ref[outers + o : outers + o + 1, :] = jnp.sum(
            named[at], axis=0, keepdims=True
        ).astype(jnp.int32)
    device = (lane & (outers - 1)) * owned + lax.div(lane, outers) * OWN
    common_ref[0:1, :] = jnp.sum(jnp.where(row == device, guests, 0.0), axis=0, keepdims=True)
    common_ref[1:2, :] = jnp.broadcast_to(failed.astype(jnp.float32), (1, LANES))


def plan(parent_slot, embedding_parent_index, rank, outers, nodes):
    slots = parent_slot.shape[0]
    return pl.pallas_call(
        functools.partial(plan_kernel, outers, nodes),
        out_shape=(
            *[pltpu.HBM((slots,), jnp.int32)] * 5,
            pltpu.HBM((2 * outers, LANES), jnp.int32),
            jax.ShapeDtypeStruct((2, LANES), jnp.float32),
        ),
        in_specs=[pl.BlockSpec(memory_space=pltpu.SMEM)]
        + [pl.BlockSpec(memory_space=pltpu.VMEM)] * 2,
        name="plan",
    )(rank, parent_slot.reshape(1, -1), embedding_parent_index.reshape(-1, LANES))


def body(embeddings, embedding_parent_index, parent_slot, centroids):
    width = embeddings.shape[1]
    children, owned, _ = centroids.shape
    nodes = lax.axis_size("node")
    outers = lax.axis_size("outer")
    devices = nodes * outers
    shrink = 1.0 / (softness_level * width)
    node = lax.axis_index("node")
    everyone = ("node", "outer")
    rank = lax.axis_index(everyone)

    me, here = rank.reshape(1), node.reshape(1)
    packed, low, unit = dense_pack(
        embeddings, parent_slot, embedding_parent_index, centroids, me, here, outers, nodes
    )
    given = (embeddings, parent_slot, embedding_parent_index)
    packed, unit, low, me, here, *given = lax.optimization_barrier(
        (packed, unit, low, me, here, *given)
    )
    arrived = lax.all_to_all(
        packed.reshape(devices, SHORT, width), everyone, split_axis=0, concat_axis=0, tiled=True
    )
    late, notes, unfit = collect(arrived, me, nodes)
    unfit, unit, low, me, here, *given = lax.optimization_barrier(
        (unfit, unit, low, me, here, *given)
    )

    def short_way():
        arrivals = lax.all_to_all(late, "node", split_axis=0, concat_axis=0, tiled=True)
        flat = low.reshape(OWN * children, width)
        total = dense_sums(arrived.reshape(devices * SHORT, width), notes, flat, shrink)
        return finish(
            total, arrivals.reshape(nodes * SHORT, width), flat, unit, here, shrink, nodes
        )

    def long_way():
        starts, counts, *_ = plan(given[1], given[2], me, outers, nodes)
        full = pack(given[0], starts, counts, outers, owned, devices)
        full = lax.all_to_all(
            full.reshape(devices, ROWS, width), everyone, split_axis=0, concat_axis=0, tiled=True
        )
        return child_sums(full.reshape(devices * ROWS, width), low, unit, shrink, nodes)

    fresh = lax.cond(unfit[0] > 0, long_way, short_way)
    received = lax.all_to_all(fresh, "node", split_axis=0, concat_axis=0, tiled=True)
    return put_in_order(received, children // nodes)


def solution(mesh):
    placed = (P(("node", "outer"), None), P(("node", "outer")), P(), P(None, "outer", None))
    return jax.shard_map(
        body,
        mesh=mesh,
        in_specs=placed,
        out_specs=(P("node", "outer", None), P("outer", None)),
        check_vma=False,
    )
```

```python
import functools

import jax
import jax.numpy as jnp
from jax import lax
from jax.experimental import pallas as pl
from jax.experimental.pallas import tpu as pltpu
from jax.sharding import PartitionSpec as P

softness_level = 0.1
prior_weight = 0.25
EPS = 1e-06

CAP = 12
OWN = 4
ROWS = OWN * CAP
TILE = 16
GROUPS = ROWS // TILE
PAIRS = 4
WIN = 32
SHORT = 32
GUESTS = 2
DENSE_PAIRS = 8
LANES = 128
NOBODY = 64


def unit_scale(values):
    return values * lax.rsqrt(jnp.mean(values * values, axis=-1, keepdims=True) + EPS)


def pack_kernel(outers, owned, start_ref, count_ref, rows_ref, out_ref, unit_ref):
    total, width = rows_ref.shape
    step = pl.program_id(0)
    chunk = 64

    @pl.when(step == 0)
    def _():
        unit_ref[total:, :] = jnp.zeros((unit_ref.shape[0] - total, width), jnp.bfloat16)

        def normalise(i, carry):
            at = pl.ds(pl.multiple_of(i * chunk, chunk), chunk)
            unit_ref[at, :] = unit_scale(rows_ref[at, :].astype(jnp.float32)).astype(jnp.bfloat16)
            return carry

        lax.fori_loop(0, total // chunk, normalise, 0, unroll=4)

    row = lax.broadcasted_iota(jnp.int32, (2 * ROWS, 1), 0)
    half = (row >= ROWS).astype(jnp.int32)
    inner = row - half * ROWS
    group = lax.shift_right_logical(inner, 4)
    place = inner & (TILE - 1)
    first = place < CAP
    source = half * OWN + jnp.where(first, group, OWN - 1)
    position = jnp.where(first, place, group * (TILE - CAP) + place - CAP)
    column = lax.broadcasted_iota(jnp.int32, (2 * ROWS, 2 * OWN * WIN), 1)
    for pair in range(PAIRS):
        target = jnp.full((2 * ROWS, 1), -1, jnp.int32)
        windows = []
        for q in range(2 * OWN):
            device = (step * PAIRS + pair) * 2 + q // OWN
            slot = lax.rem(device, outers) * owned + lax.div(device, outers) * OWN + q % OWN
            start = start_ref[slot]
            count = count_ref[slot]
            aligned = lax.shift_left(lax.shift_right_logical(start, 4), 4)
            windows.append(unit_ref[pl.ds(pl.multiple_of(aligned, TILE), WIN), :])
            spot = q * WIN + (start - aligned) + position
            target = jnp.where((source == q) & (position < count), spot, target)
        selector = (column == target).astype(jnp.float32).astype(jnp.bfloat16)
        window = jnp.concatenate(windows, axis=0)
        out_ref[pair * 2 * ROWS : (pair + 1) * 2 * ROWS, :] = jnp.dot(
            selector, window, preferred_element_type=jnp.float32
        ).astype(jnp.bfloat16)


def pack(embeddings, starts, counts, outers, owned, devices):
    total, width = embeddings.shape
    return pl.pallas_call(
        functools.partial(pack_kernel, outers, owned),
        out_shape=jax.ShapeDtypeStruct((devices * ROWS, width), jnp.bfloat16),
        grid_spec=pltpu.PrefetchScalarGridSpec(
            num_scalar_prefetch=2,
            grid=(devices // (2 * PAIRS),),
            in_specs=[
                pl.BlockSpec((total, width), lambda i, s, c: (0, 0), pipeline_mode=pl.Buffered(1))
            ],
            out_specs=pl.BlockSpec((2 * ROWS * PAIRS, width), lambda i, s, c: (i, 0)),
            scratch_shapes=[pltpu.VMEM((total + WIN, width), jnp.bfloat16)],
        ),
        compiler_params=pltpu.CompilerParams(vmem_limit_bytes=40 << 20),
        name="pack",
    )(starts, counts, embeddings)


def sums_kernel(shrink, per_node, rows_ref, low_ref, unit_ref, out_ref, total_ref):
    step = pl.program_id(0)
    block, width = rows_ref.shape
    sources = block // ROWS
    children = low_ref.shape[1]

    @pl.when(step == 0)
    def _():
        total_ref[...] = jnp.zeros_like(total_ref)

    lane = lax.broadcasted_iota(jnp.int32, (1, sources * TILE), 1)
    first = (lane & (TILE - 1)) < CAP
    for g in range(GROUPS):
        rows = jnp.concatenate(
            [rows_ref[b * ROWS + g * TILE : b * ROWS + (g + 1) * TILE, :] for b in range(sources)],
            axis=0,
        )
        low = jnp.concatenate([low_ref[g], low_ref[OWN - 1]], axis=0)
        logits = lax.dot_general(
            low, rows, (((1,), (1,)), ((), ())), preferred_element_type=jnp.float32
        )
        chosen = jnp.where(first, logits[:children], logits[children:]) * shrink
        raised = jnp.exp(chosen)
        weights = raised / jnp.sum(raised, axis=0, keepdims=True)
        zero = jnp.zeros_like(weights)
        paired = jnp.concatenate(
            [jnp.where(first, weights, zero), jnp.where(first, zero, weights)], axis=0
        ).astype(jnp.bfloat16)
        sums = jnp.dot(paired, rows, preferred_element_type=jnp.float32)
        total_ref[g] += sums[:children]
        total_ref[OWN - 1] += sums[children:]

    @pl.when(step == pl.num_programs(0) - 1)
    def _():
        parents = []
        for j in range(OWN):
            fresh = unit_scale(prior_weight * unit_ref[j] + total_ref[j])
            parents.append(unit_scale(jnp.sum(fresh, axis=0, keepdims=True)))
            fresh = fresh.astype(jnp.bfloat16)
            for m in range(children // per_node):
                out_ref[m, j * per_node : (j + 1) * per_node, :] = fresh[
                    m * per_node : (m + 1) * per_node
                ]
        tail = jnp.concatenate(parents + parents, axis=0).astype(jnp.bfloat16)
        for m in range(children // per_node):
            out_ref[m, OWN * per_node :, :] = tail


def child_sums(arrived, low, unit, shrink, nodes):
    total, width = arrived.shape
    children = low.shape[1]
    per_node = children // nodes
    block = 32 * ROWS
    whole = lambda i: (0, 0, 0)
    return pl.pallas_call(
        functools.partial(sums_kernel, shrink, per_node),
        out_shape=jax.ShapeDtypeStruct((nodes, OWN * per_node + 2 * OWN, width), jnp.bfloat16),
        grid=(total // block,),
        in_specs=[
            pl.BlockSpec((block, width), lambda i: (i, 0)),
            pl.BlockSpec(low.shape, whole, pipeline_mode=pl.Buffered(1)),
            pl.BlockSpec(unit.shape, whole, pipeline_mode=pl.Buffered(1)),
        ],
        out_specs=pl.BlockSpec((nodes, OWN * per_node + 2 * OWN, width), whole),
        scratch_shapes=[pltpu.VMEM((OWN, children, width), jnp.float32)],
        compiler_params=pltpu.CompilerParams(vmem_limit_bytes=48 << 20),
        name="child_sums",
    )(arrived, low, unit)


def order_kernel(per_node, rows_ref, children_ref, parents_ref):
    block = OWN * per_node + 2 * OWN
    nodes = rows_ref.shape[0] // block
    slots = nodes * OWN
    column = lax.broadcasted_iota(jnp.int32, (1, rows_ref.shape[0]), 1)
    out = lax.broadcasted_iota(jnp.int32, (per_node * slots, 1), 0)
    slot = out & (slots - 1)
    child = lax.div(out, slots)
    wanted = lax.div(slot, OWN) * block + (slot & (OWN - 1)) * per_node + child
    mover = (wanted == column).astype(jnp.float32).astype(jnp.bfloat16)
    rows = rows_ref[...]
    children_ref[...] = jnp.dot(mover, rows, preferred_element_type=jnp.float32)
    slot = lax.broadcasted_iota(jnp.int32, (slots, 1), 0)
    wanted = lax.div(slot, OWN) * block + OWN * per_node + (slot & (OWN - 1))
    mover = (wanted == column).astype(jnp.float32).astype(jnp.bfloat16)
    parents_ref[...] = jnp.dot(mover, rows, preferred_element_type=jnp.float32)


def put_in_order(received, per_node):
    nodes, block, width = received.shape
    slots = nodes * OWN
    children, parents = pl.pallas_call(
        functools.partial(order_kernel, per_node),
        out_shape=(
            jax.ShapeDtypeStruct((per_node * slots, width), jnp.float32),
            jax.ShapeDtypeStruct((slots, width), jnp.float32),
        ),
        name="put_in_order",
    )(received.reshape(nodes * block, width))
    return children.reshape(per_node, slots, width), parents


def dense_pack_kernel(
    outers,
    owned,
    nodes,
    me_ref,
    node_ref,
    slot_ref,
    ids_ref,
    far_rows_ref,
    centroid_ref,
    out_ref,
    low_ref,
    unit_ref,
    rows_ref,
    wide_ref,
    common_ref,
    *work,
):
    planned, placed, done = work[:6], work[6:12], work[12]
    start_ref, count_ref, guests_ref, turn_ref, hosts_ref, spill_ref = placed
    total, width = rows_ref.shape
    step = pl.program_id(0)

    @pl.when(step == 0)
    def _():
        fetch = pltpu.make_async_copy(far_rows_ref, rows_ref, done.at[len(placed)])
        fetch.start()
        plan_kernel(outers, nodes, me_ref, slot_ref, ids_ref, *planned, common_ref)

    outer_bits = outers.bit_length() - 1
    centroids = centroid_ref[...].astype(jnp.float32).reshape(wide_ref.shape[1], width)
    for c in range(width // LANES):
        wide_ref[c] = centroids[:, c * LANES : (c + 1) * LANES]
    for j in range(OWN):
        at = OWN * (node_ref[0] & 1) + j
        few = wide_ref.shape[1] // 8
        mine = [wide_ref[c, pl.ds(at, few, stride=8), :] for c in range(width // LANES)]
        unit = unit_scale(jnp.concatenate(mine, axis=1))
        unit_ref[j] = unit
        low_ref[j] = unit.astype(jnp.bfloat16)

    @pl.when(step == 0)
    def _():
        copies = [
            pltpu.make_async_copy(planned[i], placed[i], done.at[i]) for i in range(len(placed))
        ]
        for copy in copies:
            copy.start()
        for copy in copies:
            copy.wait()
        pltpu.make_async_copy(far_rows_ref, rows_ref, done.at[len(placed)]).wait()

    place = lax.broadcasted_iota(jnp.int32, (SHORT, 1), 0) - 1
    column = lax.broadcasted_iota(jnp.int32, (SHORT, 2 * OWN * WIN), 1)
    lane = lax.broadcasted_iota(jnp.int32, (1, LANES), 1)
    lane_place = (lane & (SHORT - 1)) - 1
    top = lax.broadcasted_iota(jnp.int32, (8, 1), 0) == 0
    filler = jnp.zeros((1, width - 3 * LANES), jnp.float32)
    notes = jnp.concatenate([common_ref[0:1, :], common_ref[1:2, :], filler], axis=1)
    for pair in range(DENSE_PAIRS):
        windows = []
        selectors = []
        heads = []
        for h in range(2):
            device = (step * DENSE_PAIRS + pair) * 2 + h
            base = (device & (outers - 1)) * owned + (device >> outer_bits) * OWN
            at = jnp.int32(0)
            target = jnp.full((SHORT, 1), -1, jnp.int32)
            slots = jnp.full((1, LANES), NOBODY, jnp.int32)
            for j in range(OWN):
                start = start_ref[base + j]
                aligned = lax.shift_left(lax.shift_right_logical(start, 4), 4)
                aligned = jnp.minimum(aligned, total - WIN)
                windows.append(rows_ref[pl.ds(pl.multiple_of(aligned, TILE), WIN), :])
                count = count_ref[base + j]
                if j == OWN - 1:
                    target = jnp.where(place < at, target, -1)
                    slots = jnp.where(lane_place < at, slots, NOBODY)
                    sent = jnp.minimum(at + count, SHORT - 1)
                    last = jnp.where(sent > SHORT - 1 - GUESTS, SHORT - 1, SHORT - 1 - GUESTS)
                    at = at + last - sent
                spot = (h * OWN + j) * WIN + (start - aligned) - at
                target = jnp.where(place >= at, place + spot, target)
                slots = jnp.where(lane_place >= at, j, slots)
                at = at + count
            at = jnp.minimum(at, last)
            target = jnp.where(place < at, target, -1)
            slots = jnp.where(lane_place < at, slots, NOBODY)
            selectors.append(jnp.where(column == target, 1.0, 0.0).astype(jnp.bfloat16))
            heads.append(jnp.concatenate([slots.astype(jnp.float32), notes], axis=1))
        moved = unit_scale(
            jnp.dot(
                jnp.concatenate(selectors, axis=0),
                jnp.concatenate(windows, axis=0),
                preferred_element_type=jnp.float32,
            )
        )
        pieces = []
        for h in range(2):
            pieces.append(jnp.where(top, heads[h], moved[h * SHORT : h * SHORT + 8]))
            pieces.append(moved[h * SHORT + 8 : (h + 1) * SHORT])
        out_ref[pair * 2 * SHORT : (pair + 1) * 2 * SHORT, :] = jnp.concatenate(
            pieces, axis=0
        ).astype(jnp.bfloat16)

    tile_row = lax.broadcasted_iota(jnp.int32, (TILE, 1), 0)

    def base_of(m):
        device = step * 2 * DENSE_PAIRS + m
        return (device & (outers - 1)) * owned + (device >> outer_bits) * OWN

    def seat(m, base, i):
        outer = lax.shift_right_logical(base, owned.bit_length() - 1)
        entry = turn_ref[base] + i * hosts_ref[base]
        source = spill_ref[outer, entry]
        slot = spill_ref[outers + outer, entry].astype(jnp.float32)
        aligned = lax.shift_left(lax.shift_right_logical(source, 4), 4)
        tile = rows_ref[pl.ds(pl.multiple_of(aligned, TILE), TILE), :].astype(jnp.float32)
        chosen = unit_scale(
            jnp.sum(jnp.where(tile_row == source - aligned, tile, 0.0), axis=0, keepdims=True)
        )
        tail = slice(m * SHORT + TILE, (m + 1) * SHORT)
        kept = out_ref[tail, :].astype(jnp.float32)
        out_ref[tail, :] = jnp.where(tile_row == TILE - 1 - i, chosen, kept).astype(jnp.bfloat16)
        head = slice(m * SHORT, m * SHORT + TILE)
        where = slice(3 * LANES, 4 * LANES)
        kept = out_ref[head, where].astype(jnp.float32)
        mine = (tile_row == 0) & ((lane & 7) == 7 - i)
        out_ref[head, where] = jnp.where(mine, slot, kept).astype(jnp.bfloat16)

    bases = [base_of(m) for m in range(2 * DENSE_PAIRS)]
    seated = guests_ref[bases[0]]
    for base in bases[1:]:
        seated = seated + guests_ref[base]

    @pl.when(seated > 0)
    def _():
        for m, base in enumerate(bases):
            guests = guests_ref[base]

            @pl.when(guests > 0)
            def _():
                seat(m, base, 0)

                @pl.when(guests > 1)
                def _():
                    seat(m, base, 1)


def dense_pack(embeddings, parent_slot, ids, centroids, me, node, outers, nodes):
    total, width = embeddings.shape
    children, owned, _ = centroids.shape
    slots = parent_slot.shape[0]
    devices = outers * nodes
    block = 2 * SHORT * DENSE_PAIRS
    steps = devices // (2 * DENSE_PAIRS)
    few = children // steps
    finished = pl.BlockSpec((OWN, few, width), lambda i, *_: (0, i, 0))
    shapes = [(slots,)] * 5 + [(2 * outers, LANES)]
    return pl.pallas_call(
        functools.partial(dense_pack_kernel, outers, owned, nodes),
        out_shape=(
            pltpu.HBM((devices * SHORT, width), jnp.bfloat16),
            jax.ShapeDtypeStruct((OWN, children, width), jnp.bfloat16),
            jax.ShapeDtypeStruct((OWN, children, width), jnp.float32),
        ),
        grid_spec=pltpu.PrefetchScalarGridSpec(
            num_scalar_prefetch=2,
            grid=(steps,),
            in_specs=[
                pl.BlockSpec((1, slots), lambda i, *_: (0, 0), pipeline_mode=pl.Buffered(1)),
                pl.BlockSpec(
                    (total // LANES, LANES), lambda i, *_: (0, 0), pipeline_mode=pl.Buffered(1)
                ),
                pl.BlockSpec(memory_space=pltpu.HBM),
                pl.BlockSpec((few, 8, width), lambda i, m, n: (i, n[0] >> 1, 0)),
            ],
            out_specs=(pl.BlockSpec((block, width), lambda i, *_: (i, 0)), finished, finished),
            scratch_shapes=[
                pltpu.VMEM((total, width), jnp.bfloat16),
                pltpu.VMEM((width // LANES, few * 8, LANES), jnp.float32),
                pltpu.VMEM((2, LANES), jnp.float32),
                *[pltpu.VMEM(shape, jnp.int32) for shape in shapes],
                *[pltpu.SMEM(shape, jnp.int32) for shape in shapes],
                pltpu.SemaphoreType.DMA((len(shapes) + 1,)),
            ],
        ),
        compiler_params=pltpu.CompilerParams(vmem_limit_bytes=62 << 20),
        name="dense_pack",
    )(me, node, parent_slot.reshape(1, -1), ids.reshape(-1, LANES), embeddings, centroids)


def collect_kernel(me_ref, rows_ref, head_ref, late_ref, notes_ref, unfit_ref, wide_ref):
    sources = rows_ref.shape[0]
    width = rows_ref.shape[2]
    columns = sources * 8
    heads = head_ref[...].astype(jnp.float32).reshape(sources * 8, head_ref.shape[2])
    notes = []
    for q in range(wide_ref.shape[0]):
        wide_ref[q] = heads[:, q * LANES : (q + 1) * LANES]
        notes.append(wide_ref[q, pl.ds(0, sources, stride=8), :])
    notes = jnp.concatenate(notes, axis=1)
    notes_ref[...] = notes[:, :LANES]
    everyone = notes[:, LANES : 2 * LANES]
    crowded = jnp.max(jnp.sum(everyone, axis=0, keepdims=True)) > SHORT - 1
    failed = jnp.max(notes[:, 2 * LANES : 3 * LANES]) > 0.0
    unfit_ref[0] = (crowded | failed).astype(jnp.int32)

    lane = lax.broadcasted_iota(jnp.int32, (1, LANES), 1)
    guests = jnp.sum(jnp.where(lane == me_ref[0], everyone, 0.0), axis=1, keepdims=True)
    column = lax.broadcasted_iota(jnp.int32, (1, columns), 1)
    owner = lax.shift_right_logical(column, 3)
    source = lax.broadcasted_iota(jnp.int32, (sources, 1), 0)
    before = jnp.sum(jnp.where(source < owner, guests, 0.0), axis=0, keepdims=True)
    here = jnp.sum(jnp.where(source == owner, guests, 0.0), axis=0, keepdims=True)
    slots = jnp.concatenate([notes[:, 3 * LANES :]] * (columns // LANES), axis=1)
    slots = jnp.sum(jnp.where(source == owner, slots, 0.0), axis=0, keepdims=True)
    order = 7 - (column & 7)
    place = jnp.where(order < here.astype(jnp.int32), before.astype(jnp.int32) + order + 1, -1)
    wanted = lax.broadcasted_iota(jnp.int32, (LANES, 1), 0) & (SHORT - 1)
    selector = (wanted == place).astype(jnp.float32).astype(jnp.bfloat16)
    slots = jnp.broadcast_to(slots, (8, columns)).astype(jnp.bfloat16)
    head = lax.dot_general(
        slots, selector, (((1,), (1,)), ((), ())), preferred_element_type=jnp.float32
    )[0:1]
    head = jnp.concatenate([head] * (width // LANES), axis=1)
    rows = rows_ref[...].astype(jnp.float32).reshape(columns, width).astype(jnp.bfloat16)
    moved = jnp.dot(selector[:SHORT], rows, preferred_element_type=jnp.float32)
    top = lax.broadcasted_iota(jnp.int32, (SHORT, 1), 0) == 0
    moved = jnp.where(top, head, moved).astype(jnp.bfloat16)
    for n in range(late_ref.shape[0]):
        late_ref[n] = moved


def collect(arrived, me, nodes):
    sources, short, width = arrived.shape
    return pl.pallas_call(
        collect_kernel,
        out_shape=(
            jax.ShapeDtypeStruct((nodes, SHORT, width), jnp.bfloat16),
            jax.ShapeDtypeStruct((sources, LANES), jnp.float32),
            jax.ShapeDtypeStruct((1,), jnp.int32),
        ),
        grid_spec=pltpu.PrefetchScalarGridSpec(
            num_scalar_prefetch=1,
            grid=(1,),
            in_specs=[
                pl.BlockSpec((sources, 8, width), lambda i, m: (0, short // 8 - 1, 0)),
                pl.BlockSpec((sources, 8, 4 * LANES), lambda i, m: (0, 0, 0)),
            ],
            out_specs=(
                pl.BlockSpec((nodes, SHORT, width), lambda i, m: (0, 0, 0)),
                pl.BlockSpec((sources, LANES), lambda i, m: (0, 0)),
                pl.BlockSpec(memory_space=pltpu.SMEM),
            ),
            scratch_shapes=[pltpu.VMEM((4, sources * 8, LANES), jnp.float32)],
        ),
        compiler_params=pltpu.CompilerParams(vmem_limit_bytes=58 << 20),
        name="collect",
    )(me, arrived, arrived)


def weighted_rows(low, rows, slots, shrink, piece, owners=OWN):
    children = low.shape[0] // owners
    spread = []
    for at in range(0, rows.shape[0], piece):
        here = slots[:, at : at + piece]
        logits = lax.dot_general(
            low,
            rows[at : at + piece],
            (((1,), (1,)), ((), ())),
            preferred_element_type=jnp.float32,
        )
        chosen = jnp.zeros((children, piece), jnp.float32)
        for j in range(owners):
            chosen = jnp.where(here == j, logits[j * children : (j + 1) * children], chosen)
        raised = jnp.exp(chosen * shrink)
        weights = raised / jnp.sum(raised, axis=0, keepdims=True)
        spread.append(
            jnp.concatenate(
                [jnp.where(here == j, weights, 0.0) for j in range(owners)], axis=0
            ).astype(jnp.bfloat16)
        )
    spread = jnp.concatenate(spread, axis=1)
    return jnp.dot(spread, rows, preferred_element_type=jnp.float32)


def along_lanes(notes):
    count = notes.shape[0]
    column = lax.broadcasted_iota(jnp.int32, (1, count * SHORT), 1)
    source = lax.broadcasted_iota(jnp.int32, (count, 1), 0)
    wide = jnp.concatenate([notes] * (count * SHORT // LANES), axis=1)
    mine = source == lax.shift_right_logical(column, 5)
    return jnp.sum(jnp.where(mine, wide, 0.0), axis=0, keepdims=True).astype(jnp.int32)


def dense_sums_kernel(shrink, rows_ref, notes_ref, low_ref, total_ref):
    half = pl.program_id(1)
    sources, _, tile, width = rows_ref.shape
    children = low_ref.shape[0] // OWN
    rows = rows_ref[...].reshape(sources * tile, width)
    notes = notes_ref[...]
    lane = lax.broadcasted_iota(jnp.int32, (1, LANES), 1)
    notes = jnp.where((lax.shift_right_logical(lane, 4) & 1) == half, notes, pltpu.roll(notes, 16, 1))
    column = lax.broadcasted_iota(jnp.int32, (1, sources * tile), 1)
    source = lax.broadcasted_iota(jnp.int32, (sources, 1), 0)
    wide = jnp.concatenate([notes] * (sources * tile // LANES), axis=1)
    mine = source == lax.shift_right_logical(column, 4)
    slots = jnp.sum(jnp.where(mine, wide, 0.0), axis=0, keepdims=True).astype(jnp.int32)
    at = pl.ds(pl.multiple_of(half * children, children), (OWN - 1) * children)
    sums = weighted_rows(low_ref[at, :], rows, slots - half, shrink, 256, OWN - 1)

    @pl.when((pl.program_id(0) == 0) & (half == 0))
    def _():
        total_ref[...] = jnp.zeros_like(total_ref)

    total_ref[at, :] += sums


def dense_sums(arrived, notes, low, shrink):
    sources, short, width = arrived.shape
    total = sources * short
    some = 64
    return pl.pallas_call(
        functools.partial(dense_sums_kernel, shrink),
        out_shape=jax.ShapeDtypeStruct(low.shape, jnp.float32),
        grid=(sources // some, short // TILE),
        in_specs=[
            pl.BlockSpec((some, 1, TILE, width), lambda i, h: (i, h, 0, 0)),
            pl.BlockSpec((some, LANES), lambda i, h: (i, 0)),
            pl.BlockSpec(low.shape, lambda i, h: (0, 0), pipeline_mode=pl.Buffered(1)),
        ],
        out_specs=pl.BlockSpec(low.shape, lambda i, h: (0, 0)),
        compiler_params=pltpu.CompilerParams(vmem_limit_bytes=48 << 20),
        cost_estimate=pl.CostEstimate(
            flops=4 * total * width * low.shape[0],
            bytes_accessed=2 * total * width + 6 * low.size,
            transcendentals=total * low.shape[0] // OWN,
        ),
        name="dense_sums",
    )(arrived.reshape(sources, short // TILE, TILE, width), notes, low)


def finish_kernel(shrink, per_node, node_ref, total_ref, late_ref, low_ref, unit_ref, out_ref):
    children = unit_ref.shape[1]
    late = late_ref.shape[0] // SHORT
    notes = jnp.concatenate(
        [
            late_ref[b * SHORT : b * SHORT + TILE, :LANES].astype(jnp.float32)[0:1]
            for b in range(late)
        ],
        axis=0,
    )
    slots = along_lanes(notes) - 1 - OWN * node_ref[0]
    added = weighted_rows(low_ref[...], late_ref[...], slots, shrink, 256)
    parents = []
    for j in range(OWN):
        at = slice(j * children, (j + 1) * children)
        fresh = unit_scale(prior_weight * unit_ref[j] + (total_ref[at, :] + added[at]))
        parents.append(unit_scale(jnp.sum(fresh, axis=0, keepdims=True)))
        fresh = fresh.astype(jnp.bfloat16)
        for m in range(children // per_node):
            out_ref[m, j * per_node : (j + 1) * per_node, :] = fresh[
                m * per_node : (m + 1) * per_node
            ]
    tail = jnp.concatenate(parents + parents, axis=0).astype(jnp.bfloat16)
    for m in range(children // per_node):
        out_ref[m, OWN * per_node :, :] = tail


def finish(total, late, low, unit, node, shrink, nodes):
    per_node = unit.shape[1] // nodes
    out = (nodes, OWN * per_node + 2 * OWN, late.shape[1])
    return pl.pallas_call(
        functools.partial(finish_kernel, shrink, per_node),
        out_shape=jax.ShapeDtypeStruct(out, jnp.bfloat16),
        in_specs=[pl.BlockSpec(memory_space=pltpu.SMEM)]
        + [pl.BlockSpec(memory_space=pltpu.VMEM)] * 4,
        compiler_params=pltpu.CompilerParams(vmem_limit_bytes=48 << 20),
        name="finish",
    )(node, total, late, low, unit)


def plan_kernel(
    outers,
    nodes,
    rank_ref,
    slot_ref,
    ids_ref,
    start_ref,
    count_ref,
    guests_ref,
    turn_ref,
    hosts_ref,
    spill_ref,
    common_ref,
):
    slots = slot_ref.shape[1]
    owned = slots // outers
    blocks = ids_ref.shape[0]
    room = SHORT - 1
    wide = (slots, LANES)
    row = lax.broadcasted_iota(jnp.int32, wide, 0)
    lane = lax.broadcasted_iota(jnp.int32, wide, 1)
    rows = row.astype(jnp.float32)
    ones = jnp.ones((LANES, LANES), jnp.bfloat16)

    def flag(mask):
        return jnp.where(mask, 1.0, 0.0).astype(jnp.bfloat16)

    def times(left, right):
        return jnp.dot(left, right.astype(jnp.bfloat16), preferred_element_type=jnp.float32)

    ids = jnp.concatenate(
        [
            ids_ref[...].astype(jnp.float32),
            jnp.full((LANES - blocks, LANES), slots, jnp.float32),
        ],
        axis=0,
    )
    last = jnp.broadcast_to(jnp.transpose(ids)[LANES - 1 :, :], (8, LANES))
    previous = pltpu.roll(last, 1, 1)[0:1]
    last = last[0:1]
    full = last < rows
    reached = (lane == 0) | (previous < rows)
    block = flag(reached & (last >= rows))
    upper = jnp.floor(ids * 0.5)
    inside = times(block, jnp.concatenate([upper, ids - 2.0 * upper], axis=1))
    inside = 2.0 * inside[:, :LANES] + inside[:, LANES:]
    begins = LANES * times(flag(full), ones) + times(flag(inside < rows), ones)
    ends = pltpu.roll(begins, slots - 1, 0)
    ends = jnp.where(row == slots - 1, float(blocks * LANES), ends)

    other = lax.broadcasted_iota(jnp.int32, (slots, slots), 0)
    mover = flag(slot_ref[...] == other)
    upper = jnp.floor(begins * (1.0 / TILE))
    moved = times(mover, jnp.concatenate([upper, begins - TILE * upper], axis=1))
    starts = TILE * moved[:, :LANES] + moved[:, LANES:]
    counts = times(mover, ends - begins)

    def within(mask, *values):
        parts = range(0, slots, LANES)
        side = [value[at : at + LANES] for value in values for at in parts]
        sums = times(flag(mask), jnp.concatenate(side, axis=1))
        sums = [sums[:, at : at + LANES] for at in range(0, sums.shape[1], LANES)]
        each = len(parts)
        return [
            jnp.concatenate(sums[v * each : (v + 1) * each], axis=0) for v in range(len(values))
        ]

    one = lax.broadcasted_iota(jnp.int32, (LANES, LANES), 0)
    two = lax.broadcasted_iota(jnp.int32, (LANES, LANES), 1)
    group_one, group_two = lax.shift_right_logical(one, 2), lax.shift_right_logical(two, 2)
    same_group = group_one == group_two
    same_outer = lax.div(one, owned) == lax.div(two, owned)
    (first,) = within(same_group & (two < one), counts)
    (sent,) = within(same_group, counts)
    over = jnp.maximum(sent - room, 0.0)
    host = jnp.where(sent <= room - GUESTS, 1.0, 0.0)
    once = jnp.where((row & (OWN - 1)) == 0, 1.0, 0.0)
    parts = (over * once, host * once)
    over_first, host_first = within(same_outer & (group_two < group_one), *parts)
    overs, real_hosts = within(same_outer, *parts)
    hosts = jnp.maximum(real_hosts, 1.0)
    shift = jnp.zeros_like(hosts)
    for h in range(1, nodes + 1):
        shift = jnp.where(hosts == h, lax.rem(rank_ref[0], h).astype(jnp.float32), shift)
    turn = host_first - shift
    turn = jnp.where(turn < 0.0, turn + hosts, turn)
    guests = host * (
        jnp.where(overs > turn, 1.0, 0.0) + jnp.where(overs > turn + hosts, 1.0, 0.0)
    )
    failed = jnp.max(overs - GUESTS * real_hosts) > 0.0

    flat = jnp.zeros(wide, jnp.float32)
    for q, value in enumerate([starts, counts, guests, turn, hosts]):
        flat = jnp.where(lane == q, value, flat)
    flat = jnp.transpose(flat)[:8].astype(jnp.int32)
    for q, ref in enumerate([start_ref, count_ref, guests_ref, turn_ref, hosts_ref]):
        ref[...] = flat[q : q + 1].reshape(slots)

    begin = over_first + jnp.maximum(first - room, 0.0)
    end = over_first + jnp.maximum(first + counts - room, 0.0)
    entry = lane.astype(jnp.float32)
    held = (begin <= entry) & (entry < end)
    source = jnp.where(held, starts - first + room - over_first + entry, 0.0)
    named = jnp.where(held, ((row & (owned - 1)) + 1).astype(jnp.float32), 0.0)
    for o in range(outers):
        at = slice(o * owned, (o + 1) * owned)
        spill_ref[o : o + 1, :] = jnp.sum(source[at], axis=0, keepdims=True).astype(jnp.int32)
        spill_ref[outers + o : outers + o + 1, :] = jnp.sum(
            named[at], axis=0, keepdims=True
        ).astype(jnp.int32)
    device = (lane & (outers - 1)) * owned + lax.div(lane, outers) * OWN
    common_ref[0:1, :] = jnp.sum(jnp.where(row == device, guests, 0.0), axis=0, keepdims=True)
    common_ref[1:2, :] = jnp.broadcast_to(failed.astype(jnp.float32), (1, LANES))


def plan(parent_slot, embedding_parent_index, rank, outers, nodes):
    slots = parent_slot.shape[0]
    return pl.pallas_call(
        functools.partial(plan_kernel, outers, nodes),
        out_shape=(
            *[pltpu.HBM((slots,), jnp.int32)] * 5,
            pltpu.HBM((2 * outers, LANES), jnp.int32),
            jax.ShapeDtypeStruct((2, LANES), jnp.float32),
        ),
        in_specs=[pl.BlockSpec(memory_space=pltpu.SMEM)]
        + [pl.BlockSpec(memory_space=pltpu.VMEM)] * 2,
        name="plan",
    )(rank, parent_slot.reshape(1, -1), embedding_parent_index.reshape(-1, LANES))


def body(embeddings, embedding_parent_index, parent_slot, centroids):
    width = embeddings.shape[1]
    children, owned, _ = centroids.shape
    nodes = lax.axis_size("node")
    outers = lax.axis_size("outer")
    devices = nodes * outers
    shrink = 1.0 / (softness_level * width)
    node = lax.axis_index("node")
    everyone = ("node", "outer")
    rank = lax.axis_index(everyone)

    me, here = rank.reshape(1), node.reshape(1)
    packed, low, unit = dense_pack(
        embeddings, parent_slot, embedding_parent_index, centroids, me, here, outers, nodes
    )
    given = (embeddings, parent_slot, embedding_parent_index)
    packed, unit, low, me, here, *given = lax.optimization_barrier(
        (packed, unit, low, me, here, *given)
    )
    arrived = lax.all_to_all(
        packed.reshape(devices, SHORT, width), everyone, split_axis=0, concat_axis=0, tiled=True
    )
    late, notes, unfit = collect(arrived, me, nodes)
    unfit, unit, low, me, here, *given = lax.optimization_barrier(
        (unfit, unit, low, me, here, *given)
    )

    def short_way():
        arrivals = lax.all_to_all(late, "node", split_axis=0, concat_axis=0, tiled=True)
        flat = low.reshape(OWN * children, width)
        total = dense_sums(arrived, notes, flat, shrink)
        return finish(
            total, arrivals.reshape(nodes * SHORT, width), flat, unit, here, shrink, nodes
        )

    def long_way():
        starts, counts, *_ = plan(given[1], given[2], me, outers, nodes)
        full = pack(given[0], starts, counts, outers, owned, devices)
        full = lax.all_to_all(
            full.reshape(devices, ROWS, width), everyone, split_axis=0, concat_axis=0, tiled=True
        )
        return child_sums(full.reshape(devices * ROWS, width), low, unit, shrink, nodes)

    fresh = lax.cond(unfit[0] > 0, long_way, short_way)
    received = lax.all_to_all(fresh, "node", split_axis=0, concat_axis=0, tiled=True)
    return put_in_order(received, children // nodes)


def solution(mesh):
    placed = (P(("node", "outer"), None), P(("node", "outer")), P(), P(None, "outer", None))
    return jax.shard_map(
        body,
        mesh=mesh,
        in_specs=placed,
        out_specs=(P("node", "outer", None), P("outer", None)),
        check_vma=False,
    )
```

```python
import functools

import jax
import jax.numpy as jnp
from jax import lax
from jax.experimental import pallas as pl
from jax.experimental.pallas import tpu as pltpu
from jax.sharding import PartitionSpec as P

softness_level = 0.1
prior_weight = 0.25
EPS = 1e-06

CAP = 12
OWN = 4
ROWS = OWN * CAP
TILE = 16
GROUPS = ROWS // TILE
PAIRS = 4
WIN = 32
SHORT = 32
GUESTS = 2
DENSE_PAIRS = 8
LANES = 128
NOBODY = 64


def unit_scale(values):
    return values * lax.rsqrt(jnp.mean(values * values, axis=-1, keepdims=True) + EPS)


def pack_kernel(outers, owned, start_ref, count_ref, rows_ref, out_ref, unit_ref):
    total, width = rows_ref.shape
    step = pl.program_id(0)
    chunk = 64

    @pl.when(step == 0)
    def _():
        unit_ref[total:, :] = jnp.zeros((unit_ref.shape[0] - total, width), jnp.bfloat16)

        def normalise(i, carry):
            at = pl.ds(pl.multiple_of(i * chunk, chunk), chunk)
            unit_ref[at, :] = unit_scale(rows_ref[at, :].astype(jnp.float32)).astype(jnp.bfloat16)
            return carry

        lax.fori_loop(0, total // chunk, normalise, 0, unroll=4)

    row = lax.broadcasted_iota(jnp.int32, (2 * ROWS, 1), 0)
    half = (row >= ROWS).astype(jnp.int32)
    inner = row - half * ROWS
    group = lax.shift_right_logical(inner, 4)
    place = inner & (TILE - 1)
    first = place < CAP
    source = half * OWN + jnp.where(first, group, OWN - 1)
    position = jnp.where(first, place, group * (TILE - CAP) + place - CAP)
    column = lax.broadcasted_iota(jnp.int32, (2 * ROWS, 2 * OWN * WIN), 1)
    for pair in range(PAIRS):
        target = jnp.full((2 * ROWS, 1), -1, jnp.int32)
        windows = []
        for q in range(2 * OWN):
            device = (step * PAIRS + pair) * 2 + q // OWN
            slot = lax.rem(device, outers) * owned + lax.div(device, outers) * OWN + q % OWN
            start = start_ref[slot]
            count = count_ref[slot]
            aligned = lax.shift_left(lax.shift_right_logical(start, 4), 4)
            windows.append(unit_ref[pl.ds(pl.multiple_of(aligned, TILE), WIN), :])
            spot = q * WIN + (start - aligned) + position
            target = jnp.where((source == q) & (position < count), spot, target)
        selector = (column == target).astype(jnp.float32).astype(jnp.bfloat16)
        window = jnp.concatenate(windows, axis=0)
        out_ref[pair * 2 * ROWS : (pair + 1) * 2 * ROWS, :] = jnp.dot(
            selector, window, preferred_element_type=jnp.float32
        ).astype(jnp.bfloat16)


def pack(embeddings, starts, counts, outers, owned, devices):
    total, width = embeddings.shape
    return pl.pallas_call(
        functools.partial(pack_kernel, outers, owned),
        out_shape=jax.ShapeDtypeStruct((devices * ROWS, width), jnp.bfloat16),
        grid_spec=pltpu.PrefetchScalarGridSpec(
            num_scalar_prefetch=2,
            grid=(devices // (2 * PAIRS),),
            in_specs=[
                pl.BlockSpec((total, width), lambda i, s, c: (0, 0), pipeline_mode=pl.Buffered(1))
            ],
            out_specs=pl.BlockSpec((2 * ROWS * PAIRS, width), lambda i, s, c: (i, 0)),
            scratch_shapes=[pltpu.VMEM((total + WIN, width), jnp.bfloat16)],
        ),
        compiler_params=pltpu.CompilerParams(vmem_limit_bytes=40 << 20),
        name="pack",
    )(starts, counts, embeddings)


def sums_kernel(shrink, per_node, rows_ref, low_ref, unit_ref, out_ref, total_ref):
    step = pl.program_id(0)
    block, width = rows_ref.shape
    sources = block // ROWS
    children = low_ref.shape[1]

    @pl.when(step == 0)
    def _():
        total_ref[...] = jnp.zeros_like(total_ref)

    lane = lax.broadcasted_iota(jnp.int32, (1, sources * TILE), 1)
    first = (lane & (TILE - 1)) < CAP
    for g in range(GROUPS):
        rows = jnp.concatenate(
            [rows_ref[b * ROWS + g * TILE : b * ROWS + (g + 1) * TILE, :] for b in range(sources)],
            axis=0,
        )
        low = jnp.concatenate([low_ref[g], low_ref[OWN - 1]], axis=0)
        logits = lax.dot_general(
            low, rows, (((1,), (1,)), ((), ())), preferred_element_type=jnp.float32
        )
        chosen = jnp.where(first, logits[:children], logits[children:]) * shrink
        raised = jnp.exp(chosen)
        weights = raised / jnp.sum(raised, axis=0, keepdims=True)
        zero = jnp.zeros_like(weights)
        paired = jnp.concatenate(
            [jnp.where(first, weights, zero), jnp.where(first, zero, weights)], axis=0
        ).astype(jnp.bfloat16)
        sums = jnp.dot(paired, rows, preferred_element_type=jnp.float32)
        total_ref[g] += sums[:children]
        total_ref[OWN - 1] += sums[children:]

    @pl.when(step == pl.num_programs(0) - 1)
    def _():
        parents = []
        for j in range(OWN):
            fresh = unit_scale(prior_weight * unit_ref[j] + total_ref[j])
            parents.append(unit_scale(jnp.sum(fresh, axis=0, keepdims=True)))
            fresh = fresh.astype(jnp.bfloat16)
            for m in range(children // per_node):
                out_ref[m, j * per_node : (j + 1) * per_node, :] = fresh[
                    m * per_node : (m + 1) * per_node
                ]
        tail = jnp.concatenate(parents + parents, axis=0).astype(jnp.bfloat16)
        for m in range(children // per_node):
            out_ref[m, OWN * per_node :, :] = tail


def child_sums(arrived, low, unit, shrink, nodes):
    total, width = arrived.shape
    children = low.shape[1]
    per_node = children // nodes
    block = 32 * ROWS
    whole = lambda i: (0, 0, 0)
    return pl.pallas_call(
        functools.partial(sums_kernel, shrink, per_node),
        out_shape=jax.ShapeDtypeStruct((nodes, OWN * per_node + 2 * OWN, width), jnp.bfloat16),
        grid=(total // block,),
        in_specs=[
            pl.BlockSpec((block, width), lambda i: (i, 0)),
            pl.BlockSpec(low.shape, whole, pipeline_mode=pl.Buffered(1)),
            pl.BlockSpec(unit.shape, whole, pipeline_mode=pl.Buffered(1)),
        ],
        out_specs=pl.BlockSpec((nodes, OWN * per_node + 2 * OWN, width), whole),
        scratch_shapes=[pltpu.VMEM((OWN, children, width), jnp.float32)],
        compiler_params=pltpu.CompilerParams(vmem_limit_bytes=48 << 20),
        name="child_sums",
    )(arrived, low, unit)


def order_kernel(per_node, rows_ref, children_ref, parents_ref):
    block = OWN * per_node + 2 * OWN
    nodes = rows_ref.shape[0] // block
    slots = nodes * OWN
    column = lax.broadcasted_iota(jnp.int32, (1, rows_ref.shape[0]), 1)
    out = lax.broadcasted_iota(jnp.int32, (per_node * slots, 1), 0)
    slot = out & (slots - 1)
    child = lax.div(out, slots)
    wanted = lax.div(slot, OWN) * block + (slot & (OWN - 1)) * per_node + child
    mover = (wanted == column).astype(jnp.float32).astype(jnp.bfloat16)
    rows = rows_ref[...]
    children_ref[...] = jnp.dot(mover, rows, preferred_element_type=jnp.float32)
    slot = lax.broadcasted_iota(jnp.int32, (slots, 1), 0)
    wanted = lax.div(slot, OWN) * block + OWN * per_node + (slot & (OWN - 1))
    mover = (wanted == column).astype(jnp.float32).astype(jnp.bfloat16)
    parents_ref[...] = jnp.dot(mover, rows, preferred_element_type=jnp.float32)


def put_in_order(received, per_node):
    nodes, block, width = received.shape
    slots = nodes * OWN
    children, parents = pl.pallas_call(
        functools.partial(order_kernel, per_node),
        out_shape=(
            jax.ShapeDtypeStruct((per_node * slots, width), jnp.float32),
            jax.ShapeDtypeStruct((slots, width), jnp.float32),
        ),
        name="put_in_order",
    )(received.reshape(nodes * block, width))
    return children.reshape(per_node, slots, width), parents


def dense_pack_kernel(
    outers,
    owned,
    nodes,
    me_ref,
    node_ref,
    slot_ref,
    ids_ref,
    far_rows_ref,
    centroid_ref,
    out_ref,
    low_ref,
    unit_ref,
    rows_ref,
    wide_ref,
    common_ref,
    *work,
):
    planned, placed, done = work[:6], work[6:12], work[12]
    start_ref, count_ref, guests_ref, turn_ref, hosts_ref, spill_ref = placed
    total, width = rows_ref.shape
    step = pl.program_id(0)

    @pl.when(step == 0)
    def _():
        fetch = pltpu.make_async_copy(far_rows_ref, rows_ref, done.at[len(placed)])
        fetch.start()
        plan_kernel(outers, nodes, me_ref, slot_ref, ids_ref, *planned, common_ref)

    outer_bits = outers.bit_length() - 1
    centroids = centroid_ref[...].astype(jnp.float32).reshape(wide_ref.shape[1], width)
    for c in range(width // LANES):
        wide_ref[c] = centroids[:, c * LANES : (c + 1) * LANES]
    for j in range(OWN):
        at = OWN * (node_ref[0] & 1) + j
        few = wide_ref.shape[1] // 8
        mine = [wide_ref[c, pl.ds(at, few, stride=8), :] for c in range(width // LANES)]
        unit = unit_scale(jnp.concatenate(mine, axis=1))
        unit_ref[j] = unit
        low_ref[j] = unit.astype(jnp.bfloat16)

    @pl.when(step == 0)
    def _():
        copies = [
            pltpu.make_async_copy(planned[i], placed[i], done.at[i]) for i in range(len(placed))
        ]
        for copy in copies:
            copy.start()
        for copy in copies:
            copy.wait()
        pltpu.make_async_copy(far_rows_ref, rows_ref, done.at[len(placed)]).wait()

    place = lax.broadcasted_iota(jnp.int32, (SHORT, 1), 0) - 1
    column = lax.broadcasted_iota(jnp.int32, (SHORT, 2 * OWN * WIN), 1)
    lane = lax.broadcasted_iota(jnp.int32, (1, LANES), 1)
    lane_place = (lane & (SHORT - 1)) - 1
    top = lax.broadcasted_iota(jnp.int32, (8, 1), 0) == 0
    filler = jnp.zeros((1, width - 3 * LANES), jnp.float32)
    notes = jnp.concatenate([common_ref[0:1, :], common_ref[1:2, :], filler], axis=1)
    for pair in range(DENSE_PAIRS):
        windows = []
        selectors = []
        heads = []
        for h in range(2):
            device = (step * DENSE_PAIRS + pair) * 2 + h
            base = (device & (outers - 1)) * owned + (device >> outer_bits) * OWN
            at = jnp.int32(0)
            target = jnp.full((SHORT, 1), -1, jnp.int32)
            slots = jnp.full((1, LANES), NOBODY, jnp.int32)
            for j in range(OWN):
                start = start_ref[base + j]
                aligned = lax.shift_left(lax.shift_right_logical(start, 4), 4)
                aligned = jnp.minimum(aligned, total - WIN)
                windows.append(rows_ref[pl.ds(pl.multiple_of(aligned, TILE), WIN), :])
                count = count_ref[base + j]
                if j == OWN - 1:
                    target = jnp.where(place < at, target, -1)
                    slots = jnp.where(lane_place < at, slots, NOBODY)
                    sent = jnp.minimum(at + count, SHORT - 1)
                    last = jnp.where(sent > SHORT - 1 - GUESTS, SHORT - 1, SHORT - 1 - GUESTS)
                    at = at + last - sent
                spot = (h * OWN + j) * WIN + (start - aligned) - at
                target = jnp.where(place >= at, place + spot, target)
                slots = jnp.where(lane_place >= at, j, slots)
                at = at + count
            at = jnp.minimum(at, last)
            target = jnp.where(place < at, target, -1)
            slots = jnp.where(lane_place < at, slots, NOBODY)
            selectors.append(jnp.where(column == target, 1.0, 0.0).astype(jnp.bfloat16))
            heads.append(jnp.concatenate([slots.astype(jnp.float32), notes], axis=1))
        moved = unit_scale(
            jnp.dot(
                jnp.concatenate(selectors, axis=0),
                jnp.concatenate(windows, axis=0),
                preferred_element_type=jnp.float32,
            )
        )
        pieces = []
        for h in range(2):
            pieces.append(jnp.where(top, heads[h], moved[h * SHORT : h * SHORT + 8]))
            pieces.append(moved[h * SHORT + 8 : (h + 1) * SHORT])
        out_ref[pair * 2 * SHORT : (pair + 1) * 2 * SHORT, :] = jnp.concatenate(
            pieces, axis=0
        ).astype(jnp.bfloat16)

    tile_row = lax.broadcasted_iota(jnp.int32, (TILE, 1), 0)

    def base_of(m):
        device = step * 2 * DENSE_PAIRS + m
        return (device & (outers - 1)) * owned + (device >> outer_bits) * OWN

    def seat(m, base, i):
        outer = lax.shift_right_logical(base, owned.bit_length() - 1)
        entry = turn_ref[base] + i * hosts_ref[base]
        source = spill_ref[outer, entry]
        slot = spill_ref[outers + outer, entry].astype(jnp.float32)
        aligned = lax.shift_left(lax.shift_right_logical(source, 4), 4)
        tile = rows_ref[pl.ds(pl.multiple_of(aligned, TILE), TILE), :].astype(jnp.float32)
        chosen = unit_scale(
            jnp.sum(jnp.where(tile_row == source - aligned, tile, 0.0), axis=0, keepdims=True)
        )
        tail = slice(m * SHORT + TILE, (m + 1) * SHORT)
        kept = out_ref[tail, :].astype(jnp.float32)
        out_ref[tail, :] = jnp.where(tile_row == TILE - 1 - i, chosen, kept).astype(jnp.bfloat16)
        head = slice(m * SHORT, m * SHORT + TILE)
        where = slice(3 * LANES, 4 * LANES)
        kept = out_ref[head, where].astype(jnp.float32)
        mine = (tile_row == 0) & ((lane & 7) == 7 - i)
        out_ref[head, where] = jnp.where(mine, slot, kept).astype(jnp.bfloat16)

    bases = [base_of(m) for m in range(2 * DENSE_PAIRS)]
    seated = guests_ref[bases[0]]
    for base in bases[1:]:
        seated = seated + guests_ref[base]

    @pl.when(seated > 0)
    def _():
        for m, base in enumerate(bases):
            guests = guests_ref[base]

            @pl.when(guests > 0)
            def _():
                seat(m, base, 0)

                @pl.when(guests > 1)
                def _():
                    seat(m, base, 1)


def dense_pack(embeddings, parent_slot, ids, centroids, me, node, outers, nodes):
    total, width = embeddings.shape
    children, owned, _ = centroids.shape
    slots = parent_slot.shape[0]
    devices = outers * nodes
    block = 2 * SHORT * DENSE_PAIRS
    steps = devices // (2 * DENSE_PAIRS)
    few = children // steps
    finished = pl.BlockSpec((OWN, few, width), lambda i, *_: (0, i, 0))
    shapes = [(slots,)] * 5 + [(2 * outers, LANES)]
    return pl.pallas_call(
        functools.partial(dense_pack_kernel, outers, owned, nodes),
        out_shape=(
            pltpu.HBM((devices * SHORT, width), jnp.bfloat16),
            jax.ShapeDtypeStruct((OWN, children, width), jnp.bfloat16),
            jax.ShapeDtypeStruct((OWN, children, width), jnp.float32),
        ),
        grid_spec=pltpu.PrefetchScalarGridSpec(
            num_scalar_prefetch=2,
            grid=(steps,),
            in_specs=[
                pl.BlockSpec((1, slots), lambda i, *_: (0, 0), pipeline_mode=pl.Buffered(1)),
                pl.BlockSpec(
                    (total // LANES, LANES), lambda i, *_: (0, 0), pipeline_mode=pl.Buffered(1)
                ),
                pl.BlockSpec(memory_space=pltpu.HBM),
                pl.BlockSpec((few, 8, width), lambda i, m, n: (i, n[0] >> 1, 0)),
            ],
            out_specs=(pl.BlockSpec((block, width), lambda i, *_: (i, 0)), finished, finished),
            scratch_shapes=[
                pltpu.VMEM((total, width), jnp.bfloat16),
                pltpu.VMEM((width // LANES, few * 8, LANES), jnp.float32),
                pltpu.VMEM((2, LANES), jnp.float32),
                *[pltpu.VMEM(shape, jnp.int32) for shape in shapes],
                *[pltpu.SMEM(shape, jnp.int32) for shape in shapes],
                pltpu.SemaphoreType.DMA((len(shapes) + 1,)),
            ],
        ),
        compiler_params=pltpu.CompilerParams(vmem_limit_bytes=62 << 20),
        name="dense_pack",
    )(me, node, parent_slot.reshape(1, -1), ids.reshape(-1, LANES), embeddings, centroids)


def collect_kernel(me_ref, rows_ref, head_ref, late_ref, notes_ref, unfit_ref, wide_ref):
    sources = rows_ref.shape[0]
    width = rows_ref.shape[2]
    columns = sources * 8
    heads = head_ref[...].astype(jnp.float32).reshape(sources * 8, head_ref.shape[2])
    notes = []
    for q in range(wide_ref.shape[0]):
        wide_ref[q] = heads[:, q * LANES : (q + 1) * LANES]
        notes.append(wide_ref[q, pl.ds(0, sources, stride=8), :])
    notes = jnp.concatenate(notes, axis=1)
    notes_ref[...] = notes[:, :LANES]
    everyone = notes[:, LANES : 2 * LANES]
    crowded = jnp.max(jnp.sum(everyone, axis=0, keepdims=True)) > SHORT - 1
    failed = jnp.max(notes[:, 2 * LANES : 3 * LANES]) > 0.0
    unfit_ref[0] = (crowded | failed).astype(jnp.int32)

    lane = lax.broadcasted_iota(jnp.int32, (1, LANES), 1)
    guests = jnp.sum(jnp.where(lane == me_ref[0], everyone, 0.0), axis=1, keepdims=True)
    column = lax.broadcasted_iota(jnp.int32, (1, columns), 1)
    owner = lax.shift_right_logical(column, 3)
    source = lax.broadcasted_iota(jnp.int32, (sources, 1), 0)
    before = jnp.sum(jnp.where(source < owner, guests, 0.0), axis=0, keepdims=True)
    here = jnp.sum(jnp.where(source == owner, guests, 0.0), axis=0, keepdims=True)
    slots = jnp.concatenate([notes[:, 3 * LANES :]] * (columns // LANES), axis=1)
    slots = jnp.sum(jnp.where(source == owner, slots, 0.0), axis=0, keepdims=True)
    order = 7 - (column & 7)
    place = jnp.where(order < here.astype(jnp.int32), before.astype(jnp.int32) + order + 1, -1)
    wanted = lax.broadcasted_iota(jnp.int32, (LANES, 1), 0) & (SHORT - 1)
    selector = (wanted == place).astype(jnp.float32).astype(jnp.bfloat16)
    slots = jnp.broadcast_to(slots, (8, columns)).astype(jnp.bfloat16)
    head = lax.dot_general(
        slots, selector, (((1,), (1,)), ((), ())), preferred_element_type=jnp.float32
    )[0:1]
    head = jnp.concatenate([head] * (width // LANES), axis=1)
    rows = rows_ref[...].astype(jnp.float32).reshape(columns, width).astype(jnp.bfloat16)
    moved = jnp.dot(selector[:SHORT], rows, preferred_element_type=jnp.float32)
    top = lax.broadcasted_iota(jnp.int32, (SHORT, 1), 0) == 0
    moved = jnp.where(top, head, moved).astype(jnp.bfloat16)
    for n in range(late_ref.shape[0]):
        late_ref[n] = moved


def collect(arrived, me, nodes):
    sources, short, width = arrived.shape
    return pl.pallas_call(
        collect_kernel,
        out_shape=(
            jax.ShapeDtypeStruct((nodes, SHORT, width), jnp.bfloat16),
            jax.ShapeDtypeStruct((sources, LANES), jnp.float32),
            jax.ShapeDtypeStruct((1,), jnp.int32),
        ),
        grid_spec=pltpu.PrefetchScalarGridSpec(
            num_scalar_prefetch=1,
            grid=(1,),
            in_specs=[
                pl.BlockSpec((sources, 8, width), lambda i, m: (0, short // 8 - 1, 0)),
                pl.BlockSpec((sources, 8, 4 * LANES), lambda i, m: (0, 0, 0)),
            ],
            out_specs=(
                pl.BlockSpec((nodes, SHORT, width), lambda i, m: (0, 0, 0)),
                pl.BlockSpec((sources, LANES), lambda i, m: (0, 0)),
                pl.BlockSpec(memory_space=pltpu.SMEM),
            ),
            scratch_shapes=[pltpu.VMEM((4, sources * 8, LANES), jnp.float32)],
        ),
        compiler_params=pltpu.CompilerParams(vmem_limit_bytes=58 << 20),
        name="collect",
    )(me, arrived, arrived)


def weighted_rows(low, rows, slots, shrink, piece, owners=OWN):
    children = low.shape[0] // owners
    spread = []
    for at in range(0, rows.shape[0], piece):
        here = slots[:, at : at + piece]
        logits = lax.dot_general(
            low,
            rows[at : at + piece],
            (((1,), (1,)), ((), ())),
            preferred_element_type=jnp.float32,
        )
        chosen = jnp.zeros((children, piece), jnp.float32)
        for j in range(owners):
            chosen = jnp.where(here == j, logits[j * children : (j + 1) * children], chosen)
        raised = jnp.exp(chosen * shrink)
        weights = raised / jnp.sum(raised, axis=0, keepdims=True)
        spread.append(
            jnp.concatenate(
                [jnp.where(here == j, weights, 0.0) for j in range(owners)], axis=0
            ).astype(jnp.bfloat16)
        )
    spread = jnp.concatenate(spread, axis=1)
    return jnp.dot(spread, rows, preferred_element_type=jnp.float32)


def along_lanes(notes):
    count = notes.shape[0]
    column = lax.broadcasted_iota(jnp.int32, (1, count * SHORT), 1)
    source = lax.broadcasted_iota(jnp.int32, (count, 1), 0)
    wide = jnp.concatenate([notes] * (count * SHORT // LANES), axis=1)
    mine = source == lax.shift_right_logical(column, 5)
    return jnp.sum(jnp.where(mine, wide, 0.0), axis=0, keepdims=True).astype(jnp.int32)


def dense_sums_kernel(shrink, rows_ref, notes_ref, low_ref, total_ref):
    half = pl.program_id(1)
    sources, _, tile, width = rows_ref.shape
    children = low_ref.shape[0] // OWN
    rows = rows_ref[...].reshape(sources * tile, width)
    notes = notes_ref[...]
    lane = lax.broadcasted_iota(jnp.int32, (1, LANES), 1)
    notes = jnp.where((lax.shift_right_logical(lane, 4) & 1) == half, notes, pltpu.roll(notes, 16, 1))
    column = lax.broadcasted_iota(jnp.int32, (1, sources * tile), 1)
    source = lax.broadcasted_iota(jnp.int32, (sources, 1), 0)
    wide = jnp.concatenate([notes] * (sources * tile // LANES), axis=1)
    mine = source == lax.shift_right_logical(column, 4)
    slots = jnp.sum(jnp.where(mine, wide, 0.0), axis=0, keepdims=True).astype(jnp.int32)
    at = pl.ds(pl.multiple_of(half * children, children), (OWN - 1) * children)
    sums = weighted_rows(low_ref[at, :], rows, slots - half, shrink, 256, OWN - 1)

    @pl.when((pl.program_id(0) == 0) & (half == 0))
    def _():
        total_ref[: (OWN - 1) * children, :] = sums
        total_ref[(OWN - 1) * children :, :] = jnp.zeros((children, width), jnp.float32)

    @pl.when((pl.program_id(0) > 0) | (half > 0))
    def _():
        total_ref[at, :] += sums


def dense_sums(arrived, notes, low, shrink):
    sources, short, width = arrived.shape
    total = sources * short
    some = 128
    return pl.pallas_call(
        functools.partial(dense_sums_kernel, shrink),
        out_shape=jax.ShapeDtypeStruct(low.shape, jnp.float32),
        grid=(sources // some, short // TILE),
        in_specs=[
            pl.BlockSpec((some, 1, TILE, width), lambda i, h: (i, h, 0, 0)),
            pl.BlockSpec((some, LANES), lambda i, h: (i, 0)),
            pl.BlockSpec(low.shape, lambda i, h: (0, 0), pipeline_mode=pl.Buffered(1)),
        ],
        out_specs=pl.BlockSpec(low.shape, lambda i, h: (0, 0)),
        compiler_params=pltpu.CompilerParams(vmem_limit_bytes=48 << 20),
        cost_estimate=pl.CostEstimate(
            flops=4 * total * width * low.shape[0],
            bytes_accessed=2 * total * width + 6 * low.size,
            transcendentals=total * low.shape[0] // OWN,
        ),
        name="dense_sums",
    )(arrived.reshape(sources, short // TILE, TILE, width), notes, low)


def finish_kernel(shrink, per_node, node_ref, total_ref, late_ref, low_ref, unit_ref, out_ref):
    children = unit_ref.shape[1]
    late = late_ref.shape[0] // SHORT
    notes = jnp.concatenate(
        [
            late_ref[b * SHORT : b * SHORT + TILE, :LANES].astype(jnp.float32)[0:1]
            for b in range(late)
        ],
        axis=0,
    )
    slots = along_lanes(notes) - 1 - OWN * node_ref[0]
    added = weighted_rows(low_ref[...], late_ref[...], slots, shrink, 256)
    parents = []
    for j in range(OWN):
        at = slice(j * children, (j + 1) * children)
        fresh = unit_scale(prior_weight * unit_ref[j] + (total_ref[at, :] + added[at]))
        parents.append(unit_scale(jnp.sum(fresh, axis=0, keepdims=True)))
        fresh = fresh.astype(jnp.bfloat16)
        for m in range(children // per_node):
            out_ref[m, j * per_node : (j + 1) * per_node, :] = fresh[
                m * per_node : (m + 1) * per_node
            ]
    tail = jnp.concatenate(parents + parents, axis=0).astype(jnp.bfloat16)
    for m in range(children // per_node):
        out_ref[m, OWN * per_node :, :] = tail


def finish(total, late, low, unit, node, shrink, nodes):
    per_node = unit.shape[1] // nodes
    out = (nodes, OWN * per_node + 2 * OWN, late.shape[1])
    return pl.pallas_call(
        functools.partial(finish_kernel, shrink, per_node),
        out_shape=jax.ShapeDtypeStruct(out, jnp.bfloat16),
        in_specs=[pl.BlockSpec(memory_space=pltpu.SMEM)]
        + [pl.BlockSpec(memory_space=pltpu.VMEM)] * 4,
        compiler_params=pltpu.CompilerParams(vmem_limit_bytes=48 << 20),
        name="finish",
    )(node, total, late, low, unit)


def plan_kernel(
    outers,
    nodes,
    rank_ref,
    slot_ref,
    ids_ref,
    start_ref,
    count_ref,
    guests_ref,
    turn_ref,
    hosts_ref,
    spill_ref,
    common_ref,
):
    slots = slot_ref.shape[1]
    owned = slots // outers
    blocks = ids_ref.shape[0]
    room = SHORT - 1
    wide = (slots, LANES)
    row = lax.broadcasted_iota(jnp.int32, wide, 0)
    lane = lax.broadcasted_iota(jnp.int32, wide, 1)
    rows = row.astype(jnp.float32)
    ones = jnp.ones((LANES, LANES), jnp.bfloat16)

    def flag(mask):
        return jnp.where(mask, 1.0, 0.0).astype(jnp.bfloat16)

    def times(left, right):
        return jnp.dot(left, right.astype(jnp.bfloat16), preferred_element_type=jnp.float32)

    ids = jnp.concatenate(
        [
            ids_ref[...].astype(jnp.float32),
            jnp.full((LANES - blocks, LANES), slots, jnp.float32),
        ],
        axis=0,
    )
    last = jnp.broadcast_to(jnp.transpose(ids)[LANES - 1 :, :], (8, LANES))
    previous = pltpu.roll(last, 1, 1)[0:1]
    last = last[0:1]
    full = last < rows
    reached = (lane == 0) | (previous < rows)
    block = flag(reached & (last >= rows))
    upper = jnp.floor(ids * 0.5)
    inside = times(block, jnp.concatenate([upper, ids - 2.0 * upper], axis=1))
    inside = 2.0 * inside[:, :LANES] + inside[:, LANES:]
    begins = LANES * times(flag(full), ones) + times(flag(inside < rows), ones)
    ends = pltpu.roll(begins, slots - 1, 0)
    ends = jnp.where(row == slots - 1, float(blocks * LANES), ends)

    other = lax.broadcasted_iota(jnp.int32, (slots, slots), 0)
    mover = flag(slot_ref[...] == other)
    upper = jnp.floor(begins * (1.0 / TILE))
    moved = times(mover, jnp.concatenate([upper, begins - TILE * upper], axis=1))
    starts = TILE * moved[:, :LANES] + moved[:, LANES:]
    counts = times(mover, ends - begins)

    def within(mask, *values):
        parts = range(0, slots, LANES)
        side = [value[at : at + LANES] for value in values for at in parts]
        sums = times(flag(mask), jnp.concatenate(side, axis=1))
        sums = [sums[:, at : at + LANES] for at in range(0, sums.shape[1], LANES)]
        each = len(parts)
        return [
            jnp.concatenate(sums[v * each : (v + 1) * each], axis=0) for v in range(len(values))
        ]

    one = lax.broadcasted_iota(jnp.int32, (LANES, LANES), 0)
    two = lax.broadcasted_iota(jnp.int32, (LANES, LANES), 1)
    group_one, group_two = lax.shift_right_logical(one, 2), lax.shift_right_logical(two, 2)
    same_group = group_one == group_two
    same_outer = lax.div(one, owned) == lax.div(two, owned)
    (first,) = within(same_group & (two < one), counts)
    (sent,) = within(same_group, counts)
    over = jnp.maximum(sent - room, 0.0)
    host = jnp.where(sent <= room - GUESTS, 1.0, 0.0)
    once = jnp.where((row & (OWN - 1)) == 0, 1.0, 0.0)
    parts = (over * once, host * once)
    over_first, host_first = within(same_outer & (group_two < group_one), *parts)
    overs, real_hosts = within(same_outer, *parts)
    hosts = jnp.maximum(real_hosts, 1.0)
    shift = jnp.zeros_like(hosts)
    for h in range(1, nodes + 1):
        shift = jnp.where(hosts == h, lax.rem(rank_ref[0], h).astype(jnp.float32), shift)
    turn = host_first - shift
    turn = jnp.where(turn < 0.0, turn + hosts, turn)
    guests = host * (
        jnp.where(overs > turn, 1.0, 0.0) + jnp.where(overs > turn + hosts, 1.0, 0.0)
    )
    failed = jnp.max(overs - GUESTS * real_hosts) > 0.0

    flat = jnp.zeros(wide, jnp.float32)
    for q, value in enumerate([starts, counts, guests, turn, hosts]):
        flat = jnp.where(lane == q, value, flat)
    flat = jnp.transpose(flat)[:8].astype(jnp.int32)
    for q, ref in enumerate([start_ref, count_ref, guests_ref, turn_ref, hosts_ref]):
        ref[...] = flat[q : q + 1].reshape(slots)

    begin = over_first + jnp.maximum(first - room, 0.0)
    end = over_first + jnp.maximum(first + counts - room, 0.0)
    entry = lane.astype(jnp.float32)
    held = (begin <= entry) & (entry < end)
    source = jnp.where(held, starts - first + room - over_first + entry, 0.0)
    named = jnp.where(held, ((row & (owned - 1)) + 1).astype(jnp.float32), 0.0)
    for o in range(outers):
        at = slice(o * owned, (o + 1) * owned)
        spill_ref[o : o + 1, :] = jnp.sum(source[at], axis=0, keepdims=True).astype(jnp.int32)
        spill_ref[outers + o : outers + o + 1, :] = jnp.sum(
            named[at], axis=0, keepdims=True
        ).astype(jnp.int32)
    device = (lane & (outers - 1)) * owned + lax.div(lane, outers) * OWN
    common_ref[0:1, :] = jnp.sum(jnp.where(row == device, guests, 0.0), axis=0, keepdims=True)
    common_ref[1:2, :] = jnp.broadcast_to(failed.astype(jnp.float32), (1, LANES))


def plan(parent_slot, embedding_parent_index, rank, outers, nodes):
    slots = parent_slot.shape[0]
    return pl.pallas_call(
        functools.partial(plan_kernel, outers, nodes),
        out_shape=(
            *[pltpu.HBM((slots,), jnp.int32)] * 5,
            pltpu.HBM((2 * outers, LANES), jnp.int32),
            jax.ShapeDtypeStruct((2, LANES), jnp.float32),
        ),
        in_specs=[pl.BlockSpec(memory_space=pltpu.SMEM)]
        + [pl.BlockSpec(memory_space=pltpu.VMEM)] * 2,
        name="plan",
    )(rank, parent_slot.reshape(1, -1), embedding_parent_index.reshape(-1, LANES))


def body(embeddings, embedding_parent_index, parent_slot, centroids):
    width = embeddings.shape[1]
    children, owned, _ = centroids.shape
    nodes = lax.axis_size("node")
    outers = lax.axis_size("outer")
    devices = nodes * outers
    shrink = 1.0 / (softness_level * width)
    node = lax.axis_index("node")
    everyone = ("node", "outer")
    rank = lax.axis_index(everyone)

    me, here = rank.reshape(1), node.reshape(1)
    packed, low, unit = dense_pack(
        embeddings, parent_slot, embedding_parent_index, centroids, me, here, outers, nodes
    )
    given = (embeddings, parent_slot, embedding_parent_index)
    packed, unit, low, me, here, *given = lax.optimization_barrier(
        (packed, unit, low, me, here, *given)
    )
    arrived = lax.all_to_all(
        packed.reshape(devices, SHORT, width), everyone, split_axis=0, concat_axis=0, tiled=True
    )
    late, notes, unfit = collect(arrived, me, nodes)
    unfit, unit, low, me, here, *given = lax.optimization_barrier(
        (unfit, unit, low, me, here, *given)
    )

    def short_way():
        arrivals = lax.all_to_all(late, "node", split_axis=0, concat_axis=0, tiled=True)
        flat = low.reshape(OWN * children, width)
        total = dense_sums(arrived, notes, flat, shrink)
        return finish(
            total, arrivals.reshape(nodes * SHORT, width), flat, unit, here, shrink, nodes
        )

    def long_way():
        starts, counts, *_ = plan(given[1], given[2], me, outers, nodes)
        full = pack(given[0], starts, counts, outers, owned, devices)
        full = lax.all_to_all(
            full.reshape(devices, ROWS, width), everyone, split_axis=0, concat_axis=0, tiled=True
        )
        return child_sums(full.reshape(devices * ROWS, width), low, unit, shrink, nodes)

    fresh = lax.cond(unfit[0] > 0, long_way, short_way)
    received = lax.all_to_all(fresh, "node", split_axis=0, concat_axis=0, tiled=True)
    return put_in_order(received, children // nodes)


def solution(mesh):
    placed = (P(("node", "outer"), None), P(("node", "outer")), P(), P(None, "outer", None))
    return jax.shard_map(
        body,
        mesh=mesh,
        in_specs=placed,
        out_specs=(P("node", "outer", None), P("outer", None)),
        check_vma=False,
    )
```
